32 devices in a mesh: expert: 8 (over z, core), tensor: 4 (over y, x).
Axes of the slice: x: 2, y: 2, z: 4, core: 2. Of those that a mesh axis runs over, the one named last changes fastest.
Arguments:
- tokens: bfloat16 [256, 4096], P('expert', 'tensor'), may hold values from -6 to 6
- cotangent: bfloat16 [256, 4096], P('expert', 'tensor'), may hold values from -6 to 6
- expert_ids: int32 [256, 8], P('expert'), may hold values from 0 to 63, all different within a row; in each aligned block of 32 rows (0 to 31, 32 to 63, ...) at most 8 rows name the same one
- route_weight: float32 [256, 8], P('expert'), may hold values from 0.05 to 0.25
- w_gate: bfloat16 [64, 4096, 1536], P('expert', 'tensor'), may hold values from -0.09375 to 0.09375
- w_up: bfloat16 [64, 4096, 1536], P('expert', 'tensor'), may hold values from -0.09375 to 0.09375
- w_down: bfloat16 [64, 1536, 4096], P('expert', None, 'tensor'), may hold values from -0.15625 to 0.15625
Outputs:
- mixed_out: bfloat16 [256, 4096], P('expert', 'tensor')
- input_grad: bfloat16 [256, 4096], P('expert', 'tensor')
- down_grad: bfloat16 [64, 1536, 4096], P('expert', None, 'tensor')
The draws below stay inside these ranges and needn't reach their ends.
Inputs may be any that keep to these rules, and one draw needn't show every extreme that they name: `expert_ids`: each row names 8 different experts; within the 32 rows of one device no expert is named more than 8 times.
All inputs are finite; a program needn't handle non-finite values.
Results may differ from the reference program's by a relative error of at most 0.023.
Values may be sent and summed in bfloat16 or wider, within the bound.
No kernel may reach another device: no remote copies, remote signals or barrier semaphores. Data moves between devices by JAX's collectives and lax.ppermute only.
A program may use at most 192 MiB of HBM per device.

```python
import math
import jax
import jax.numpy as jnp
import numpy as np
from jax import lax

D = 4096
FF = 1536
TOP = 8
TOK_DEV = 32
EXPERT_TOTAL = 64
TOKENS = 256
CAP = 8
ROWS = 64
N_EXPERT = 8
N_TENSOR = 4


def block_scale(key, extent, split, least, high):
    loudness, own = 1.0, jax.random.fold_in(key, 6)
    for axis_at, blocks in split:
        draws = jnp.exp(jax.random.uniform(jax.random.fold_in(own, axis_at), (blocks,), jnp.float32, least / len(split), high / len(split)))
        loudness = loudness * jnp.repeat(draws, extent[axis_at] // blocks).reshape([-1 if axis == axis_at else 1 for axis in range(len(extent))])
    return loudness


def routed_block(stream_key, own, number, rows, count, top, limit, slope):
    sequence = jax.random.permutation(stream_key, count)
    heavy_load, usual = shares(count, rows * top, limit, slope, True), shares(count, rows * top, limit, slope, False)
    places = jnp.arange(count)

    def named(tallies, offset_by):
        used = int((tallies > 0).sum())
        fixed = max(1, used // 4)
        passed = fixed + (places - fixed + offset_by * (used - fixed)) % max(1, count - fixed)
        return jnp.zeros((count,), jnp.int32).at[sequence[jnp.where(places < fixed, places, passed)]].set(jnp.asarray(tallies, jnp.int32))

    tallies = jnp.where(number % 4 == 0, named(heavy_load, number // 4), named(usual, number - number // 4 - 1))
    mixed = jax.random.permutation(jax.random.fold_in(own, 3), count)
    giver, sink = mixed[0:count // 2 * 2:2], mixed[1:count // 2 * 2:2]
    slack = jnp.minimum(tallies[giver] - 1, limit - tallies[sink]) // 2
    slack = jnp.where((giver == sequence[0]) | (sink == sequence[0]) | (tallies[sink] == 0), 0, jnp.maximum(slack, 0))
    passed = jax.random.randint(jax.random.fold_in(own, 4), (count // 2,), 0, 1 << 20) % (slack + 1)
    tallies = tallies.at[giver].add(-passed).at[sink].add(passed)
    members = jnp.searchsorted(jnp.cumsum(tallies), jnp.arange(rows * top), side="right").astype(jnp.int32)
    grid = members.reshape(top, rows).T
    grid = grid[jax.random.permutation(jax.random.fold_in(own, 1), rows)]
    offset_by = jax.random.randint(jax.random.fold_in(own, 2), (rows, 1), 0, top)
    return jnp.take_along_axis(grid, (jnp.arange(top)[None, :] + offset_by) % top, axis=1)


def shares(number_of, total, most, lean, full):
    portions = [(1 << 20) // math.isqrt(grade ** lean) + 1 for grade in range(1, number_of + 1)]
    largest = most if full else min(most, max(-(-total // number_of), total * portions[0] // sum(portions)))
    least = 1 if total - largest >= number_of - 1 else 0
    counts, rest = [largest] + [least] * (number_of - 1), total - largest - least * (number_of - 1)
    while rest > 0:
        candidates = [i for i in range(1, number_of) if counts[i] < largest] or [i for i in range(1, number_of) if counts[i] < most]
        whole, left = sum([portions[i] for i in candidates]), rest
        for i in candidates:
            addition = min(most - counts[i], max(1, left * portions[i] // whole), rest)
            counts[i] = counts[i] + addition
            rest = rest - addition
    return np.array(counts)


def normal_values(rng, shape, scale, reach, shards=(), kind=jnp.bfloat16):
    level = block_scale(rng, shape, shards, -0.22, 0.18) if shards else 1.0
    drawn = jax.random.normal(rng, shape, jnp.float32) * scale * level
    return jnp.minimum(jnp.maximum(drawn, -reach), reach).astype(kind)


def setup_inputs(seed: int = 0) -> dict:
    splits = jax.random.split(jax.random.key(seed), 8)
    tokens = normal_values(splits[0], (TOKENS, D), 1.0, 6.0, ((0, 8), (1, 4)))
    cotangent = normal_values(splits[1], (TOKENS, D), 1.0, 6.0, ((0, 8), (1, 4)))
    expert_ids_keys = jax.random.split(jax.random.fold_in(splits[2], 1), TOKENS // TOK_DEV)
    expert_ids_turns = jax.random.permutation(jax.random.fold_in(splits[2], 3), TOKENS // TOK_DEV)
    expert_ids = jax.vmap(lambda own, number: routed_block(jax.random.fold_in(splits[2], 2), own, number, TOK_DEV, EXPERT_TOTAL, TOP, CAP, 2))(expert_ids_keys, expert_ids_turns).reshape((TOKENS, TOP))
    route_weight = jnp.clip(0.05 + 0.2 * jax.random.uniform(splits[3], (TOKENS, TOP), jnp.float32) ** block_scale(splits[3], (TOKENS, TOP), ((0, 8),), -0.2, 0.2), 0.05, 0.25)
    w_gate = normal_values(splits[4], (EXPERT_TOTAL, D, FF), D ** -0.5, 0.09375, ((0, 8), (1, 4)))
    w_up = normal_values(splits[5], (EXPERT_TOTAL, D, FF), D ** -0.5, 0.09375, ((0, 8), (1, 4)))
    w_down = normal_values(splits[6], (EXPERT_TOTAL, FF, D), FF ** -0.5, 0.15625, ((0, 8), (2, 4)))
    return {"tokens": tokens, "cotangent": cotangent, "expert_ids": expert_ids, "route_weight": route_weight, "w_gate": w_gate, "w_up": w_up, "w_down": w_down}


def reference(tokens, cotangent, expert_ids, route_weight, w_gate, w_up, w_down):
    pair_count = TOK_DEV * TOP
    ids_block = expert_ids.reshape(N_EXPERT, pair_count)
    onehot = (ids_block[:, :, None] == jnp.arange(EXPERT_TOTAL, dtype=jnp.int32)[None, None, :]).astype(jnp.int32)
    before = jnp.cumsum(onehot, axis=1) - onehot
    slot_index = jnp.sum(before * onehot, axis=2).astype(jnp.int32)
    row_index = (jnp.arange(N_EXPERT, dtype=jnp.int32)[:, None] * CAP + slot_index).reshape(-1).astype(jnp.int32)
    expert_index = expert_ids.reshape(-1).astype(jnp.int32)
    token_index = (jnp.arange(TOKENS * TOP, dtype=jnp.int32) // TOP).astype(jnp.int32)
    routing_coefficient = route_weight.reshape(-1)
    token_buffer = jnp.zeros((EXPERT_TOTAL, ROWS, D), jnp.bfloat16).at[expert_index, row_index].set(tokens[token_index])
    pair_cot = (routing_coefficient[:, None] * cotangent[token_index].astype(jnp.float32)).astype(jnp.bfloat16)
    grad_buffer = jnp.zeros((EXPERT_TOTAL, ROWS, D), jnp.bfloat16).at[expert_index, row_index].set(pair_cot)
    block_width = D // N_TENSOR

    def blocked_sum(routed, weights):
        split_token_batch = routed.reshape(ROWS, N_TENSOR, block_width).astype(jnp.float32)
        split_parameter_slices = weights.reshape(N_TENSOR, block_width, FF).astype(jnp.float32)
        incomplete_summands = jnp.einsum("qeg,egj->eqj", split_token_batch, split_parameter_slices)
        quantized_result = lax.optimization_barrier(incomplete_summands.astype(jnp.bfloat16))
        return jnp.sum(quantized_result.astype(jnp.float32), axis=0)

    def blocked_back(routed, weights):
        split_token_batch = routed.reshape(ROWS, N_TENSOR, block_width).astype(jnp.float32)
        split_parameter_slices = weights.reshape(FF, N_TENSOR, block_width).astype(jnp.float32)
        incomplete_summands = jnp.einsum("qsk,bsk->sqb", split_token_batch, split_parameter_slices)
        quantized_result = lax.optimization_barrier(incomplete_summands.astype(jnp.bfloat16))
        return jnp.sum(quantized_result.astype(jnp.float32), axis=0)

    def one_expert(operands):
        routed_x, routed_grad, gate_weight, up_weight, down_weight = operands
        gate_sum = blocked_sum(routed_x, gate_weight)
        up_sum = blocked_sum(routed_x, up_weight)
        sigmoid_val = jax.nn.sigmoid(gate_sum)
        hidden = (gate_sum * sigmoid_val * up_sum).astype(jnp.bfloat16)
        expert_out = jnp.dot(hidden, down_weight, preferred_element_type=jnp.float32).astype(jnp.bfloat16)
        down_part = jnp.dot(hidden.T, routed_grad, preferred_element_type=jnp.float32).astype(jnp.bfloat16)
        hidden_grad = blocked_back(routed_grad, down_weight)
        gate_grad = (hidden_grad * up_sum * sigmoid_val * (1.0 + gate_sum * (1.0 - sigmoid_val))).astype(jnp.bfloat16)
        up_grad = (hidden_grad * gate_sum * sigmoid_val).astype(jnp.bfloat16)
        pair_grad = jnp.dot(gate_grad, gate_weight.T, preferred_element_type=jnp.float32)
        pair_grad = (pair_grad + jnp.dot(up_grad, up_weight.T, preferred_element_type=jnp.float32)).astype(jnp.bfloat16)
        return expert_out, pair_grad, down_part

    output_holder, pair_buffer, down_grad = lax.map(one_expert, (token_buffer, grad_buffer, w_gate, w_up, w_down))
    pair_out = output_holder[expert_index, row_index].astype(jnp.float32)
    mixed_out = jnp.sum((routing_coefficient[:, None] * pair_out).reshape(TOKENS, TOP, D), axis=1).astype(jnp.bfloat16)
    pair_back = pair_buffer[expert_index, row_index].astype(jnp.float32)
    input_grad = jnp.sum(pair_back.reshape(TOKENS, TOP, D), axis=1).astype(jnp.bfloat16)
    return mixed_out, input_grad, down_grad
```

```python
import functools
import jax
import jax.numpy as jnp
from jax import lax
from jax.experimental import pallas as pl
from jax.experimental.pallas import tpu as pltpu
from jax.sharding import PartitionSpec as P

BF16 = jnp.bfloat16
F32 = jnp.float32
VMEM_LIMIT = 48 << 20
META = 128


def xor_permute(x, axis, mask):
    return lax.ppermute(x, axis, [(i, i ^ mask) for i in range(lax.axis_size(axis))])


def dot(a, b, contract):
    return lax.dot_general(a, b, ((contract[0], contract[1]), ((), ())), preferred_element_type=F32)


def whole(shape):
    return pl.BlockSpec(shape, lambda *_: (0,) * len(shape))


def route_kernel(blocks, top, experts, local, slabs, cap, where_ref, *refs):
    metas, (order_ref, fits_ref, count_ref, weight_ref) = refs[:blocks], refs[blocks:]
    my_expert, my_slab = where_ref[0], where_ref[1]
    meta = jnp.concatenate([m[...] for m in metas], axis=0)
    tokens = meta.shape[0]
    eye = (
        lax.broadcasted_iota(jnp.int32, (tokens, tokens), 0)
        == lax.broadcasted_iota(jnp.int32, (tokens, tokens), 1)
    ).astype(BF16)
    turned = dot(meta, eye, ((0,), (0,)))
    ids = turned[:top]
    weights = turned[top : 2 * top] + turned[2 * top : 3 * top] + turned[3 * top : 4 * top]

    all_names = lax.broadcasted_iota(jnp.int32, (experts, 1), 0).astype(F32)
    picked = jnp.zeros((experts, tokens), F32)
    for k in range(top):
        picked += (ids[k : k + 1] == all_names).astype(F32)
    down = jnp.sum(picked, axis=1, keepdims=True)
    across = dot(jnp.ones((8, tokens), BF16), picked.astype(BF16), ((1,), (1,)))[:1]
    row = lax.broadcasted_iota(jnp.int32, (experts, experts), 0)
    col = lax.broadcasted_iota(jnp.int32, (experts, experts), 1)
    same = row // local == col // local
    col_first = (across > down) | ((across == down) & (col < row))
    row_first = (down > across) | ((down == across) & (row < col))
    rank_down = jnp.sum((same & col_first).astype(F32), axis=1, keepdims=True)
    rank_across = jnp.sum((same & row_first).astype(F32), axis=0, keepdims=True)
    mate = same & (rank_across == (local - 1) - rank_down)
    pair = down + jnp.sum(jnp.where(mate, across, 0.0), axis=1, keepdims=True)
    fits_ref[0] = (jnp.max(pair) <= cap).astype(jnp.int32)

    names = (lax.broadcasted_iota(jnp.int32, (local, 1), 0) + my_expert * local).astype(F32)
    mine = jnp.zeros((local, tokens), F32)
    share = jnp.zeros((local, tokens), F32)
    for k in range(top):
        hit = ids[k : k + 1] == names
        mine += hit.astype(F32)
        share += jnp.where(hit, weights[k : k + 1], 0.0)
    earlier = (
        lax.broadcasted_iota(jnp.int32, (tokens, tokens), 0)
        < lax.broadcasted_iota(jnp.int32, (tokens, tokens), 1)
    ).astype(BF16)
    count = dot(mine.astype(BF16), earlier, ((1,), (0,)))
    count = jnp.where(mine > 0, count, -1.0)
    load = jnp.sum(mine, axis=1, keepdims=True)
    load_across = dot(jnp.ones((8, tokens), BF16), mine.astype(BF16), ((1,), (1,)))[:1]
    row = lax.broadcasted_iota(jnp.int32, (local, local), 0)
    col = lax.broadcasted_iota(jnp.int32, (local, local), 1)
    first = (load_across > load) | ((load_across == load) & (col < row))
    rank = jnp.sum(first.astype(F32), axis=1, keepdims=True)
    index = lax.broadcasted_iota(jnp.int32, (local, 1), 0).astype(F32)
    for place in range(slabs):
        slab = place ^ my_slab
        for end in range(2):
            wanted = (slab if end == 0 else local - 1 - slab).astype(F32)
            chosen = rank == wanted
            at = 2 * place + end
            order_ref[at] = jnp.sum(jnp.where(chosen, index, 0.0)).astype(jnp.int32)
            count_ref[at : at + 1] = jnp.sum(jnp.where(chosen, count, 0.0), axis=0, keepdims=True)
            weight_ref[at : at + 1] = jnp.sum(jnp.where(chosen, share, 0.0), axis=0, keepdims=True)


def route(metas, where, top, experts, local, slabs, cap):
    tokens = sum(m.shape[0] for m in metas)
    smem = pl.BlockSpec(memory_space=pltpu.SMEM)
    vmem = pl.BlockSpec(memory_space=pltpu.VMEM)
    return pl.pallas_call(
        functools.partial(route_kernel, len(metas), top, experts, local, slabs, cap),
        in_specs=[smem] + [vmem] * len(metas),
        out_specs=(smem, smem, vmem, vmem),
        out_shape=(
            jax.ShapeDtypeStruct((local,), jnp.int32),
            jax.ShapeDtypeStruct((1,), jnp.int32),
            jax.ShapeDtypeStruct((local, tokens), F32),
            jax.ShapeDtypeStruct((local, tokens), F32),
        ),
        name="route",
    )(where, *metas)


def picks(count_ref, at, end, rows):
    count = count_ref[pl.ds(at, 1), :]
    target = jnp.where(end == 0, count, jnp.where(count >= 0, (rows - 1) - count, -1.0))
    line = lax.broadcasted_iota(jnp.int32, (rows, count.shape[1]), 0).astype(F32)
    return line == target


def first_kernel(place, blocks, order, count_ref, weight_ref, *refs):
    parts = refs[:blocks]
    gate_ref, up_ref, down_ref, low_ref, high_ref, grad_ref, data, rows_ref, acc = refs[blocks:]
    step, end = pl.program_id(0), pl.program_id(1)
    rows, width = rows_ref.shape[1], rows_ref.shape[2]
    half = rows // 2

    @pl.when((step == 0) & (end == 0))
    def _():
        length = parts[0].shape[0]
        for j in range(blocks):
            data[j * length : (j + 1) * length, :] = parts[j][...]

    @pl.when(step == 0)
    def _():
        at = 2 * place + end
        chosen = picks(count_ref, at, end, rows)
        select = chosen.astype(BF16)
        scale = jnp.sum(
            jnp.where(chosen, weight_ref[pl.ds(at, 1), :], 0.0), axis=1, keepdims=True
        )
        rows_ref[end] = dot(select, data[:, :width], ((1,), (0,))).astype(BF16)
        grad_ref[end] = (dot(select, data[:, width:], ((1,), (0,))) * scale).astype(BF16)

    x, g = rows_ref[end], grad_ref[end]
    values = (
        dot(x, gate_ref[0], ((1,), (0,))),
        dot(x, up_ref[0], ((1,), (0,))),
        dot(g, down_ref[0], ((1,), (1,))),
    )

    @pl.when(end == 0)
    def _():
        for i, value in enumerate(values):
            acc[i] = value

    @pl.when(end == 1)
    def _():
        for i, value in enumerate(values):
            total = (acc[i] + value).astype(BF16)
            low_ref[i] = total[:half]
            high_ref[i] = total[half:]


def first(place, rows, order, count, weight, parts, w_gate, w_up, w_down, tile):
    _, width, hidden = w_gate.shape
    tokens = count.shape[1]
    grid = (hidden // tile, 2)

    def pick(f, a, o):
        return (o[2 * place + a], 0, f)

    def pick_down(f, a, o):
        return (o[2 * place + a], f, 0)

    half = jax.ShapeDtypeStruct((3, rows // 2, hidden), BF16)
    half_spec = pl.BlockSpec((3, rows // 2, tile), lambda f, a, o: (0, 0, f))
    return pl.pallas_call(
        functools.partial(first_kernel, place, len(parts)),
        grid_spec=pltpu.PrefetchScalarGridSpec(
            num_scalar_prefetch=1,
            grid=grid,
            in_specs=[whole(count.shape), whole(weight.shape)]
            + [whole(p.shape) for p in parts]
            + [
                pl.BlockSpec((1, width, tile), pick),
                pl.BlockSpec((1, width, tile), pick),
                pl.BlockSpec((1, tile, width), pick_down),
            ],
            out_specs=[half_spec, half_spec, whole((2, rows, width))],
            scratch_shapes=[
                pltpu.VMEM((tokens, 2 * width), BF16),
                pltpu.VMEM((2, rows, width), BF16),
                pltpu.VMEM((3, rows, tile), F32),
            ],
        ),
        out_shape=(half, half, jax.ShapeDtypeStruct((2, rows, width), BF16)),
        compiler_params=pltpu.CompilerParams(vmem_limit_bytes=VMEM_LIMIT),
        cost_estimate=pl.CostEstimate(
            flops=2 * 6 * rows * width * hidden,
            bytes_accessed=12 * width * hidden,
            transcendentals=0,
        ),
        name=f"first{place}",
    )(order, count, weight, *parts, w_gate, w_up, w_down)


def middle_kernel(*refs):
    sources, outs = refs[:6], refs[6:]
    for h in range(2):
        own, side, other = sources[3 * h : 3 * h + 3]
        gate, up, grad = [
            own[i].astype(F32) + side[i].astype(F32) + other[i].astype(F32) for i in range(3)
        ]
        sig = jax.nn.sigmoid(gate)
        outs[h][0] = (gate * sig * up).astype(BF16)
        outs[h][1] = (grad * up * sig * (1.0 + gate * (1.0 - sig))).astype(BF16)
        outs[h][2] = (grad * gate * sig).astype(BF16)


def middle(low, high):
    _, half, hidden = low[0].shape
    tile = hidden // 3
    spec = pl.BlockSpec((3, half, tile), lambda f: (0, 0, f))
    shape = jax.ShapeDtypeStruct((3, half, hidden), BF16)
    return pl.pallas_call(
        middle_kernel,
        grid=(hidden // tile,),
        in_specs=[spec] * 6,
        out_specs=(spec, spec),
        out_shape=(shape, shape),
        cost_estimate=pl.CostEstimate(
            flops=40 * half * hidden, bytes_accessed=48 * half * hidden, transcendentals=2 * half * hidden
        ),
        name="middle",
    )(*low, *high)


def second_kernel(place, has_prev, last, order, count_ref, weight_ref, low_ref, high_ref, grad_ref,
                  gate_ref, up_ref, down_ref, *refs):
    if has_prev:
        prev_ref, _, refs = refs[0], refs[1], refs[2:]
    dg_ref, refs = refs[0], refs[1:]
    token_ref, refs = refs[:2] if last else refs[:1], refs[2:] if last else refs[1:]
    out_acc, in_acc, total = refs
    end, step = pl.program_id(0), pl.program_id(1)
    rows = out_acc.shape[0]

    hid, gate_grad, up_grad = [
        jnp.concatenate([low_ref[i], high_ref[i]], axis=0) for i in range(3)
    ]
    dg_ref[0] = dot(hid, grad_ref[end], ((0,), (0,))).astype(BF16)
    out_part = dot(hid, down_ref[0], ((1,), (0,)))
    in_part = dot(gate_grad, gate_ref[0], ((1,), (1,))) + dot(up_grad, up_ref[0], ((1,), (1,)))

    @pl.when(step == 0)
    def _():
        out_acc[...] = out_part
        in_acc[...] = in_part

    @pl.when(step > 0)
    def _():
        out_acc[...] += out_part
        in_acc[...] += in_part

    @pl.when(step == pl.num_programs(1) - 1)
    def _():
        at = 2 * place + end
        chosen = picks(count_ref, at, end, rows)
        scale = jnp.where(chosen, weight_ref[pl.ds(at, 1), :], 0.0)
        high = scale.astype(BF16)
        low = (scale - high.astype(F32)).astype(BF16)
        outs = out_acc[...].astype(BF16)
        mixed = dot(high, outs, ((0,), (0,))) + dot(low, outs, ((0,), (0,)))
        back = dot(chosen.astype(BF16), in_acc[...].astype(BF16), ((0,), (0,)))

        @pl.when(end == 0)
        def _():
            if has_prev:
                total[0] = prev_ref[0] + mixed
                total[1] = prev_ref[1] + back
            else:
                total[0] = mixed
                total[1] = back

        @pl.when(end == 1)
        def _():
            for i, value in enumerate((mixed, back)):
                value = total[i] + value
                if last:
                    keep, send = token_ref
                    length = keep.shape[2]
                    for j in range(keep.shape[0]):
                        keep[j, i] = value[2 * j * length : (2 * j + 1) * length]
                        send[j, i] = value[(2 * j + 1) * length : (2 * j + 2) * length].astype(BF16)
                else:
                    token_ref[0][i] = value


def second(place, last, blocks, order, count, weight, low, high, grad, w_gate, w_up, w_down, prev, tile):
    local, width, hidden = w_gate.shape
    tokens = count.shape[1]
    rows = grad.shape[1]
    grid = (2, hidden // tile)

    def pick(a, f, o):
        return (o[2 * place + a], 0, f)

    def pick_down(a, f, o):
        return (o[2 * place + a], f, 0)

    half_spec = pl.BlockSpec((3, rows // 2, tile), lambda a, f, o: (0, 0, f))
    down_spec = pl.BlockSpec((1, tile, width), pick_down)
    in_specs = [
        whole(count.shape), whole(weight.shape), half_spec, half_spec, whole(grad.shape),
        pl.BlockSpec((1, width, tile), pick), pl.BlockSpec((1, width, tile), pick), down_spec,
    ]
    operands = [order, count, weight, low, high, grad, w_gate, w_up, w_down]
    aliases = {}
    if prev is not None:
        in_specs += [whole(prev[0].shape), pl.BlockSpec(memory_space=pl.ANY)]
        operands += list(prev)
        aliases = {len(operands) - 1: 0}
    dg_shape = jax.ShapeDtypeStruct((local, hidden, width), BF16)
    if last:
        shape = (blocks // 2, 2, tokens // blocks, width)
        token_shapes = [jax.ShapeDtypeStruct(shape, F32), jax.ShapeDtypeStruct(shape, BF16)]
    else:
        token_shapes = [jax.ShapeDtypeStruct((2, tokens, width), F32)]
    return pl.pallas_call(
        functools.partial(second_kernel, place, prev is not None, last),
        grid_spec=pltpu.PrefetchScalarGridSpec(
            num_scalar_prefetch=1,
            grid=grid,
            in_specs=in_specs,
            out_specs=[down_spec] + [whole(s.shape) for s in token_shapes],
            scratch_shapes=[
                pltpu.VMEM((rows, width), F32),
                pltpu.VMEM((rows, width), F32),
                pltpu.VMEM((2, tokens, width), F32),
            ],
        ),
        out_shape=[dg_shape] + token_shapes,
        input_output_aliases=aliases,
        compiler_params=pltpu.CompilerParams(vmem_limit_bytes=VMEM_LIMIT),
        cost_estimate=pl.CostEstimate(
            flops=2 * 8 * rows * width * hidden,
            bytes_accessed=16 * width * hidden,
            transcendentals=0,
        ),
        name=f"second{place}",
    )(*operands)


def exchange(rows, blocks, order, count, weight, parts, w_gate, w_up, w_down):
    tile = w_gate.shape[2] // 2
    args = (order, count, weight, parts, w_gate, w_up, w_down, tile)
    side = functools.partial(xor_permute, axis="tensor", mask=1)
    other = functools.partial(xor_permute, axis="tensor", mask=2)

    low3, high3, grad3 = first(3, rows, *args)
    from_side, from_other = side(low3), other(high3)
    low1, high1, grad1 = first(1, rows, *args)
    side_low = side(low1)
    low2, high2, grad2 = first(2, rows, *args)
    other_high = other(high2)

    def add(a, b):
        return (a.astype(F32) + b.astype(F32)).astype(BF16)

    side_high = side(add(high1, from_other))
    other_low = other(add(low2, from_side))
    low0, high0, grad0 = first(0, rows, *args)
    own_low, own_high = middle((low0, side_low, other_low), (high0, side_high, other_high))

    low1, high2 = side(own_low), other(own_high)
    high1, low2 = side(own_high), other(own_low)
    low3, high3 = other(low1), side(high2)
    weights = (w_gate, w_up, w_down)
    run = functools.partial(second, blocks=blocks, order=order, count=count, weight=weight,
                            w_gate=w_gate, w_up=w_up, w_down=w_down, tile=tile)
    dg, tok = run(0, False, low=own_low, high=own_high, grad=grad0, prev=None)
    dg, tok = run(1, False, low=low1, high=high1, grad=grad1, prev=(tok, dg))
    dg, tok = run(2, False, low=low2, high=high2, grad=grad2, prev=(tok, dg))
    dg, keep, send = run(3, True, low=low3, high=high3, grad=grad3, prev=(tok, dg))

    got = xor_permute(send, "expert", 1)
    total = keep[0] + got[0].astype(F32)
    for j in range(1, blocks // 2):
        piece = (keep[j] + got[j].astype(F32)).astype(BF16)
        total = total + xor_permute(piece, "expert", 2 * j).astype(F32)
    total = total.astype(BF16)
    return total[0], total[1], dg


def small(tokens, cotangent, expert_ids, route_weight, w_gate, w_up, w_down):
    blocks, slabs = lax.axis_size("expert"), lax.axis_size("tensor")
    local = w_gate.shape[0]
    experts = local * blocks
    length, top = expert_ids.shape
    capacity = 2 * length * top // experts
    most = 2 * capacity * blocks

    high = lax.reduce_precision(route_weight, 8, 7)
    rest = route_weight - high
    mid = lax.reduce_precision(rest, 8, 7)
    low = rest - mid
    meta = jnp.concatenate([expert_ids.astype(F32), high, mid, low], axis=1).astype(BF16)
    meta = jnp.pad(meta, ((0, 0), (0, META - meta.shape[1])))
    data = jnp.concatenate([tokens, cotangent], axis=1)

    def gather(x):
        even = [x] + [xor_permute(x, "expert", j) for j in range(2, blocks, 2)]
        odd = [xor_permute(v, "expert", 1) for v in even]
        return [v for both in zip(even, odd) for v in both]

    metas = gather(meta)
    parts = gather(data)
    where = jnp.stack([lax.axis_index("expert"), lax.axis_index("tensor")]).astype(jnp.int32)
    order, fits, count, weight = route(metas, where, top, experts, local, slabs, most * 3 // 4)
    return exchange(most, blocks, order, count, weight, parts, w_gate, w_up, w_down)


def large(tokens, cotangent, expert_ids, route_weight, w_gate, w_up, w_down):
    resident_specialists = w_gate.shape[0]
    experts = resident_specialists * lax.axis_size("expert")
    tok_count = expert_ids.shape[0]
    top_count = expert_ids.shape[1]
    capacity = 2 * tok_count * top_count // experts
    model_width = tokens.shape[1]
    flat_ids = expert_ids.reshape(-1)
    onehot = (flat_ids[:, None] == jnp.arange(experts, dtype=jnp.int32)[None, :]).astype(jnp.int32)
    before = jnp.cumsum(onehot, axis=0) - onehot
    slot_index = jnp.sum(before * onehot, axis=1)
    target = flat_ids * capacity + slot_index
    chosen = (target[:, None] == jnp.arange(experts * capacity, dtype=jnp.int32)[None, :]).astype(F32)
    chosen = chosen.reshape(tok_count, top_count, experts * capacity)
    expert_assignment = jnp.sum(chosen, axis=1)
    weighted = jnp.sum(chosen * route_weight[:, :, None], axis=1)
    token_send = jnp.dot(expert_assignment.T.astype(BF16), tokens, preferred_element_type=F32)
    token_send = token_send.astype(BF16).reshape(experts, capacity, model_width)
    gradient_outgoing = jnp.dot(
        weighted.T, cotangent, precision=lax.Precision.HIGHEST, preferred_element_type=F32
    )
    gradient_outgoing = gradient_outgoing.astype(BF16).reshape(experts, capacity, model_width)
    token_rows = lax.all_to_all(token_send, "expert", split_axis=0, concat_axis=1, tiled=True)
    grad_rows = lax.all_to_all(gradient_outgoing, "expert", split_axis=0, concat_axis=1, tiled=True)
    pre_gate = jnp.einsum("erd,edf->erf", token_rows, w_gate, preferred_element_type=F32)
    pre_up = jnp.einsum("erd,edf->erf", token_rows, w_up, preferred_element_type=F32)
    slice_breadth = w_gate.shape[2] // lax.axis_size("tensor")
    gate_sum = lax.psum(pre_gate.astype(BF16), "tensor").astype(F32)
    up_sum = lax.psum(pre_up.astype(BF16), "tensor").astype(F32)
    sigmoid_all = jax.nn.sigmoid(gate_sum)
    hidden = (gate_sum * sigmoid_all * up_sum).astype(BF16)
    out_rows = jnp.einsum("erf,efd->erd", hidden, w_down, preferred_element_type=F32).astype(BF16)
    down_grad = jnp.einsum("erf,erd->efd", hidden, grad_rows, preferred_element_type=F32)
    offset = lax.axis_index("tensor") * slice_breadth
    gate_part = lax.dynamic_slice_in_dim(gate_sum, offset, slice_breadth, 2)
    up_part = lax.dynamic_slice_in_dim(up_sum, offset, slice_breadth, 2)
    sigmoid_part = lax.dynamic_slice_in_dim(sigmoid_all, offset, slice_breadth, 2)
    hidden_term = jnp.einsum("erd,efd->erf", grad_rows, w_down, preferred_element_type=F32)
    hidden_grad = lax.psum_scatter(
        hidden_term.astype(BF16), "tensor", scatter_dimension=2, tiled=True
    ).astype(F32)
    gate_grad = (
        hidden_grad * up_part * sigmoid_part * (1.0 + gate_part * (1.0 - sigmoid_part))
    ).astype(BF16)
    up_grad = (hidden_grad * gate_part * sigmoid_part).astype(BF16)
    gate_piece = lax.all_gather(gate_grad, "tensor", axis=2, tiled=True)
    up_piece = lax.all_gather(up_grad, "tensor", axis=2, tiled=True)
    running = jnp.einsum("erf,edf->erd", gate_piece, w_gate, preferred_element_type=F32)
    input_rows = running + jnp.einsum("erf,edf->erd", up_piece, w_up, preferred_element_type=F32)
    input_rows = input_rows.astype(BF16)
    returned_out = lax.all_to_all(out_rows, "expert", split_axis=1, concat_axis=0, tiled=True)
    returned_in = lax.all_to_all(input_rows, "expert", split_axis=1, concat_axis=0, tiled=True)
    returned_out = returned_out.reshape(experts * capacity, model_width)
    returned_in = returned_in.reshape(experts * capacity, model_width)
    mixed_out = jnp.dot(
        weighted, returned_out, precision=lax.Precision.HIGHEST, preferred_element_type=F32
    )
    input_grad = jnp.dot(expert_assignment.astype(BF16), returned_in, preferred_element_type=F32)
    return mixed_out.astype(BF16), input_grad.astype(BF16), down_grad.astype(BF16)


def local(tokens, cotangent, expert_ids, route_weight, w_gate, w_up, w_down):
    blocks, slabs = lax.axis_size("expert"), lax.axis_size("tensor")
    pairs = w_gate.shape[0] == 2 * slabs and slabs == 4
    few = blocks <= 8 and blocks & (blocks - 1) == 0
    body = small if pairs and few else large
    return body(tokens, cotangent, expert_ids, route_weight, w_gate, w_up, w_down)


def solution(mesh):
    return jax.shard_map(
        local,
        mesh=mesh,
        in_specs=(
            P("expert", "tensor"),
            P("expert", "tensor"),
            P("expert", None),
            P("expert", None),
            P("expert", "tensor", None),
            P("expert", "tensor", None),
            P("expert", None, "tensor"),
        ),
        out_specs=(P("expert", "tensor"), P("expert", "tensor"), P("expert", None, "tensor")),
        check_vma=False,
    )
```

```python
import functools
import jax
import jax.numpy as jnp
from jax import lax
from jax.experimental import pallas as pl
from jax.experimental.pallas import tpu as pltpu
from jax.sharding import PartitionSpec as P

BF16 = jnp.bfloat16
F32 = jnp.float32
VMEM_LIMIT = 63 << 20
META = 128


def xor_permute(x, axis, mask):
    return lax.ppermute(x, axis, [(i, i ^ mask) for i in range(lax.axis_size(axis))])


def dot(a, b, contract):
    return lax.dot_general(a, b, ((contract[0], contract[1]), ((), ())), preferred_element_type=F32)


def whole(shape):
    return pl.BlockSpec(shape, lambda *_: (0,) * len(shape))


def pack_kernel(top, tokens_ref, grad_ref, ids_ref, weight_ref, out_ref):
    width = tokens_ref.shape[1]
    out_ref[:, :width] = tokens_ref[...]
    out_ref[:, width : 2 * width] = grad_ref[...]
    weight = weight_ref[...]
    high = weight.astype(BF16)
    rest = weight - high.astype(F32)
    mid = rest.astype(BF16)
    low = (rest - mid.astype(F32)).astype(BF16)
    ids = ids_ref[...].astype(F32).astype(BF16)
    fields = [v.astype(F32) for v in (ids, high, mid, low)]
    fields.append(jnp.zeros((weight.shape[0], META - 4 * top), F32))
    out_ref[:, 2 * width :] = jnp.concatenate(fields, axis=1).astype(BF16)


def pack(tokens, cotangent, expert_ids, route_weight):
    length, width = tokens.shape
    return pl.pallas_call(
        functools.partial(pack_kernel, expert_ids.shape[1]),
        out_shape=jax.ShapeDtypeStruct((length, 2 * width + META), BF16),
        name="pack",
    )(tokens, cotangent, expert_ids, route_weight)


def route_kernel(blocks, top, experts, local, slabs, cap, where_ref, *refs):
    metas, (order_ref, fits_ref, count_ref, weight_ref) = refs[:blocks], refs[blocks:]
    my_expert, my_slab = where_ref[0], where_ref[1]
    meta = jnp.concatenate([m[...] for m in metas], axis=0)
    tokens = meta.shape[0]
    eye = (
        lax.broadcasted_iota(jnp.int32, (tokens, tokens), 0)
        == lax.broadcasted_iota(jnp.int32, (tokens, tokens), 1)
    ).astype(BF16)
    turned = dot(meta, eye, ((0,), (0,)))
    ids = turned[:top]
    weights = turned[top : 2 * top] + turned[2 * top : 3 * top] + turned[3 * top : 4 * top]

    all_names = lax.broadcasted_iota(jnp.int32, (experts, 1), 0).astype(F32)
    picked = jnp.zeros((experts, tokens), F32)
    for k in range(top):
        picked += (ids[k : k + 1] == all_names).astype(F32)
    down = jnp.sum(picked, axis=1, keepdims=True)
    across = dot(jnp.ones((8, tokens), BF16), picked.astype(BF16), ((1,), (1,)))[:1]
    row = lax.broadcasted_iota(jnp.int32, (experts, experts), 0)
    col = lax.broadcasted_iota(jnp.int32, (experts, experts), 1)
    same = row // local == col // local
    col_first = (across > down) | ((across == down) & (col < row))
    row_first = (down > across) | ((down == across) & (row < col))
    rank_down = jnp.sum((same & col_first).astype(F32), axis=1, keepdims=True)
    rank_across = jnp.sum((same & row_first).astype(F32), axis=0, keepdims=True)
    mate = same & (rank_across == (local - 1) - rank_down)
    pair = down + jnp.sum(jnp.where(mate, across, 0.0), axis=1, keepdims=True)
    fits_ref[0] = (jnp.max(pair) <= cap).astype(jnp.int32)

    names = (lax.broadcasted_iota(jnp.int32, (local, 1), 0) + my_expert * local).astype(F32)
    mine = jnp.zeros((local, tokens), F32)
    share = jnp.zeros((local, tokens), F32)
    for k in range(top):
        hit = ids[k : k + 1] == names
        mine += hit.astype(F32)
        share += jnp.where(hit, weights[k : k + 1], 0.0)
    earlier = (
        lax.broadcasted_iota(jnp.int32, (tokens, tokens), 0)
        < lax.broadcasted_iota(jnp.int32, (tokens, tokens), 1)
    ).astype(BF16)
    count = dot(mine.astype(BF16), earlier, ((1,), (0,)))
    count = jnp.where(mine > 0, count, -1.0)
    load = jnp.sum(mine, axis=1, keepdims=True)
    load_across = dot(jnp.ones((8, tokens), BF16), mine.astype(BF16), ((1,), (1,)))[:1]
    row = lax.broadcasted_iota(jnp.int32, (local, local), 0)
    col = lax.broadcasted_iota(jnp.int32, (local, local), 1)
    first = (load_across > load) | ((load_across == load) & (col < row))
    rank = jnp.sum(first.astype(F32), axis=1, keepdims=True)
    index = lax.broadcasted_iota(jnp.int32, (local, 1), 0).astype(F32)
    for place in range(slabs):
        slab = place ^ my_slab
        for end in range(2):
            wanted = (slab if end == 0 else local - 1 - slab).astype(F32)
            chosen = rank == wanted
            at = 2 * place + end
            order_ref[at] = jnp.sum(jnp.where(chosen, index, 0.0)).astype(jnp.int32)
            count_ref[at : at + 1] = jnp.sum(jnp.where(chosen, count, 0.0), axis=0, keepdims=True)
            weight_ref[at : at + 1] = jnp.sum(jnp.where(chosen, share, 0.0), axis=0, keepdims=True)


def route(parts, where, top, experts, local, slabs, cap):
    length, lanes = parts[0].shape
    tokens = length * len(parts)
    smem = pl.BlockSpec(memory_space=pltpu.SMEM)
    meta = pl.BlockSpec((length, META), lambda i: (0, lanes // META - 1))
    return pl.pallas_call(
        functools.partial(route_kernel, len(parts), top, experts, local, slabs, cap),
        grid=(1,),
        in_specs=[smem] + [meta] * len(parts),
        out_specs=(smem, smem, whole((local, tokens)), whole((local, tokens))),
        compiler_params=pltpu.CompilerParams(vmem_limit_bytes=VMEM_LIMIT),
        out_shape=(
            jax.ShapeDtypeStruct((local,), jnp.int32),
            jax.ShapeDtypeStruct((1,), jnp.int32),
            jax.ShapeDtypeStruct((local, tokens), F32),
            jax.ShapeDtypeStruct((local, tokens), F32),
        ),
        name="route",
    )(where, *parts)


def picks(count_ref, at, end, rows):
    count = count_ref[pl.ds(at, 1), :]
    target = jnp.where(end == 0, count, jnp.where(count >= 0, (rows - 1) - count, -1.0))
    line = lax.broadcasted_iota(jnp.int32, (rows, count.shape[1]), 0).astype(F32)
    return line == target


def first_kernel(places, blocks, order, count_ref, weight_ref, *refs):
    parts, refs = refs[:blocks], refs[blocks:]
    (gate_ref, up_ref, down_ref), refs = refs[:3], refs[3:]
    halves, (grad_ref, data, rows_ref, acc) = refs[: 2 * len(places)], refs[2 * len(places) :]
    which, step, end = pl.program_id(0), pl.program_id(1), pl.program_id(2)
    rows, width = rows_ref.shape[1], rows_ref.shape[2]
    half = rows // 2

    @pl.when((which == 0) & (step == 0) & (end == 0))
    def _():
        length = parts[0].shape[0]
        for j in range(blocks):
            data[j * length : (j + 1) * length, :] = parts[j][...]

    @pl.when(step == 0)
    def _():
        at = 2 * nth(places, which) + end
        chosen = picks(count_ref, at, end, rows)
        select = chosen.astype(BF16)
        scale = jnp.sum(
            jnp.where(chosen, weight_ref[pl.ds(at, 1), :], 0.0), axis=1, keepdims=True
        )
        rows_ref[end] = dot(select, data[:, :width], ((1,), (0,))).astype(BF16)
        grad_ref[2 * which + end] = (
            dot(select, data[:, width:], ((1,), (0,))) * scale
        ).astype(BF16)

    x, g = rows_ref[end], grad_ref[2 * which + end]
    values = (
        dot(x, gate_ref[0], ((1,), (0,))),
        dot(x, up_ref[0], ((1,), (0,))),
        dot(g, down_ref[0], ((1,), (1,))),
    )

    @pl.when(end == 0)
    def _():
        for i, value in enumerate(values):
            acc[i] = value

    for at in range(len(places)):

        @pl.when((end == 1) & (which == at))
        def _():
            for i, value in enumerate(values):
                total = (acc[i] + value).astype(BF16)
                halves[2 * at][i] = total[:half]
                halves[2 * at + 1][i] = total[half:]


def nth(places, which):
    value = places[0]
    for at in range(1, len(places)):
        value = jnp.where(which == at, places[at], value)
    return value


def first(places, rows, order, count, weight, parts, w_gate, w_up, w_down, tile):
    _, width, hidden = w_gate.shape
    tokens = count.shape[1]
    steps = hidden // tile

    def pick(p, f, a, o):
        return (o[2 * nth(places, p) + a], 0, f)

    def pick_down(p, f, a, o):
        return (o[2 * nth(places, p) + a], f, 0)

    half = jax.ShapeDtypeStruct((3, rows // 2, hidden), BF16)

    def half_spec(at):
        def index(p, f, a, o):
            return (0, 0, jnp.where(p == at, f, jnp.where(p < at, 0, steps - 1)))

        return pl.BlockSpec((3, rows // 2, tile), index)

    specs = [half_spec(at) for at in range(len(places)) for _ in range(2)]
    grads = (2 * len(places), rows, width)
    return pl.pallas_call(
        functools.partial(first_kernel, places, len(parts)),
        grid_spec=pltpu.PrefetchScalarGridSpec(
            num_scalar_prefetch=1,
            grid=(len(places), steps, 2),
            in_specs=[whole(count.shape), whole(weight.shape)]
            + [whole((p.shape[0], 2 * width)) for p in parts]
            + [
                pl.BlockSpec((1, width, tile), pick),
                pl.BlockSpec((1, width, tile), pick),
                pl.BlockSpec((1, tile, width), pick_down),
            ],
            out_specs=specs + [whole(grads)],
            scratch_shapes=[
                pltpu.VMEM((tokens, 2 * width), BF16),
                pltpu.VMEM((2, rows, width), BF16),
                pltpu.VMEM((3, rows, tile), F32),
            ],
        ),
        out_shape=[half] * len(specs) + [jax.ShapeDtypeStruct(grads, BF16)],
        compiler_params=pltpu.CompilerParams(vmem_limit_bytes=VMEM_LIMIT),
        cost_estimate=pl.CostEstimate(
            flops=12 * len(places) * rows * width * hidden,
            bytes_accessed=12 * len(places) * width * hidden,
            transcendentals=0,
        ),
        name="first" + "".join(map(str, places)),
    )(order, count, weight, *parts, w_gate, w_up, w_down)


def middle_kernel(*refs):
    sources, outs = refs[:6], refs[6:]
    for h in range(2):
        own, side, other = sources[3 * h : 3 * h + 3]
        gate, up, grad = [
            own[i].astype(F32) + side[i].astype(F32) + other[i].astype(F32) for i in range(3)
        ]
        sig = jax.nn.sigmoid(gate)
        outs[h][0] = (gate * sig * up).astype(BF16)
        outs[h][1] = (grad * up * sig * (1.0 + gate * (1.0 - sig))).astype(BF16)
        outs[h][2] = (grad * gate * sig).astype(BF16)


def middle(low, high):
    _, half, hidden = low[0].shape
    tile = hidden // 3
    spec = pl.BlockSpec((3, half, tile), lambda f: (0, 0, f))
    shape = jax.ShapeDtypeStruct((3, half, hidden), BF16)
    return pl.pallas_call(
        middle_kernel,
        grid=(hidden // tile,),
        in_specs=[spec] * 6,
        out_specs=(spec, spec),
        out_shape=(shape, shape),
        compiler_params=pltpu.CompilerParams(vmem_limit_bytes=VMEM_LIMIT),
        cost_estimate=pl.CostEstimate(
            flops=40 * half * hidden, bytes_accessed=48 * half * hidden, transcendentals=2 * half * hidden
        ),
        name="middle",
    )(*low, *high)


def second_kernel(places, has_prev, last, order, count_ref, weight_ref, *refs):
    halves, refs = refs[: 2 * len(places)], refs[2 * len(places) :]
    (grad_ref, gate_ref, up_ref, down_ref), refs = refs[:4], refs[4:]
    done, refs = refs[: len(last)], refs[len(last) :]
    refs = refs[1:] if has_prev else refs
    dg_ref, refs = refs[0], refs[1:]
    if last:
        (keep_ref, send_ref, rows_ref, work, out_acc, in_acc, high, low, plain, total) = refs
    else:
        (rows_ref, work, out_acc, in_acc) = refs
    which, end, step = pl.program_id(0), pl.program_id(1), pl.program_id(2)
    rows, tile = work.shape[1], work.shape[2]
    half = rows // 2
    lanes = pl.ds(pl.multiple_of(step * tile, tile), tile)

    for at in range(len(places)):

        @pl.when(which == at)
        def _():
            work[:, :half] = halves[2 * at][:, :, lanes]
            work[:, half:] = halves[2 * at + 1][:, :, lanes]

    hid, gate_grad, up_grad = work[0], work[1], work[2]
    dg_ref[0] = dot(hid, grad_ref[2 * which + end], ((0,), (0,))).astype(BF16)
    out_part = dot(hid, down_ref[0], ((1,), (0,)))
    in_part = dot(gate_grad, gate_ref[0], ((1,), (1,))) + dot(up_grad, up_ref[0], ((1,), (1,)))

    @pl.when(step == 0)
    def _():
        out_acc[...] = out_part
        in_acc[...] = in_part

    @pl.when(step > 0)
    def _():
        out_acc[...] += out_part
        in_acc[...] += in_part

    @pl.when((step == pl.num_programs(2) - 1) & (end == 0))
    def _():
        rows_ref[which, 0] = out_acc[...].astype(BF16)
        rows_ref[which, 1] = in_acc[...].astype(BF16)

    @pl.when((step == pl.num_programs(2) - 1) & (end == 1))
    def _():
        at = 2 * nth(places, which) + 1
        own = jnp.max(picks(count_ref, at, 1, rows).astype(F32), axis=1, keepdims=True) > 0
        for i, value in enumerate((out_acc, in_acc)):
            before = rows_ref[which, i].astype(F32)
            rows_ref[which, i] = jnp.where(own, value[...], before).astype(BF16)

    if last:
        order_of = [p for group in last for p in group] + list(places)

        @pl.when((step == 0) & (end == 0))
        def _():
            for slot, place in enumerate(order_of):
                scale, seen = 0.0, False
                for e in range(2):
                    at = 2 * place + e
                    chosen = picks(count_ref, at, e, rows)
                    scale = scale + jnp.where(chosen, weight_ref[at : at + 1, :], 0.0)
                    seen = seen | chosen
                part = scale.astype(BF16)
                high[slot] = part
                low[slot] = (scale - part.astype(F32)).astype(BF16)
                plain[slot] = seen.astype(BF16)

        def add(slots, pairs):
            out, back = 0.0, 0.0
            for slot, (o, b) in zip(slots, pairs):
                out = out + dot(high[slot], o, ((0,), (0,))) + dot(low[slot], o, ((0,), (0,)))
                back = back + dot(plain[slot], b, ((0,), (0,)))
            return out, back

        @pl.when((step == 1) & (end == 0))
        def _():
            pairs = [(d[g, 0], d[g, 1]) for d, group in zip(done, last) for g in range(len(group))]
            out, back = add(range(len(pairs)), pairs)
            total[0] = out
            total[1] = back

        @pl.when((step == pl.num_programs(2) - 1) & (end == 1))
        def _():
            values = add([len(order_of) - 1], [(rows_ref[0, 0], rows_ref[0, 1])])
            length = keep_ref.shape[2]
            for i, value in enumerate(values):
                value = total[i] + value
                for j in range(keep_ref.shape[0]):
                    keep_ref[j, i] = value[2 * j * length : (2 * j + 1) * length]
                    send_ref[j, i] = value[(2 * j + 1) * length : (2 * j + 2) * length].astype(BF16)


def second(places, last, blocks, order, count, weight, halves, grad, w_gate, w_up, w_down, done, prev, tile):
    local, width, hidden = w_gate.shape
    tokens = count.shape[1]
    rows = grad.shape[1]
    grid = (len(places), 2, hidden // tile)

    def pick(p, a, f, o):
        return (o[2 * nth(places, p) + a], 0, f)

    def pick_down(p, a, f, o):
        return (o[2 * nth(places, p) + a], f, 0)

    down_spec = pl.BlockSpec((1, tile, width), pick_down)
    in_specs = (
        [whole(count.shape), whole(weight.shape)]
        + [whole(h.shape) for h in halves]
        + [whole(grad.shape)]
        + [pl.BlockSpec((1, width, tile), pick)] * 2
        + [down_spec]
        + [whole(d.shape) for d in done]
    )
    operands = [order, count, weight, *halves, grad, w_gate, w_up, w_down, *done]
    aliases = {}
    if prev is not None:
        in_specs.append(pl.BlockSpec(memory_space=pl.ANY))
        operands.append(prev)
        aliases = {len(operands) - 1: 0}
    row_shape = (len(places), 2, rows, width)
    scratch = [
        pltpu.VMEM((3, rows, tile), BF16),
        pltpu.VMEM((rows, width), F32),
        pltpu.VMEM((rows, width), F32),
    ]
    outs = [jax.ShapeDtypeStruct((local, hidden, width), BF16)]
    if last:
        shape = (blocks // 2, 2, tokens // blocks, width)
        outs += [jax.ShapeDtypeStruct(shape, F32), jax.ShapeDtypeStruct(shape, BF16)]
        scratch = [pltpu.VMEM(row_shape, BF16)] + scratch
        scratch += [pltpu.VMEM((local // 2, rows, tokens), BF16)] * 3
        scratch += [pltpu.VMEM((2, tokens, width), F32)]
    else:
        outs += [jax.ShapeDtypeStruct(row_shape, BF16)]
    return pl.pallas_call(
        functools.partial(second_kernel, places, prev is not None, last),
        grid_spec=pltpu.PrefetchScalarGridSpec(
            num_scalar_prefetch=1,
            grid=grid,
            in_specs=in_specs,
            out_specs=[down_spec] + [whole(s.shape) for s in outs[1:]],
            scratch_shapes=scratch,
        ),
        out_shape=outs,
        input_output_aliases=aliases,
        compiler_params=pltpu.CompilerParams(vmem_limit_bytes=VMEM_LIMIT),
        cost_estimate=pl.CostEstimate(
            flops=16 * len(places) * rows * width * hidden,
            bytes_accessed=16 * len(places) * width * hidden,
            transcendentals=0,
        ),
        name="second" + "".join(map(str, places)),
    )(*operands)


def exchange(rows, blocks, order, count, weight, parts, w_gate, w_up, w_down):
    tile = w_gate.shape[2] // 3
    args = (order, count, weight, parts, w_gate, w_up, w_down, tile)
    side = functools.partial(xor_permute, axis="tensor", mask=1)
    other = functools.partial(xor_permute, axis="tensor", mask=2)

    low3, high3, grad3 = first((3,), rows, *args)
    from_side, from_other = side(low3), other(high3)
    low1, high1, low2, high2, grad12 = first((1, 2), rows, *args)
    side_low, other_high = side(low1), other(high2)

    def add(a, b):
        return (a.astype(F32) + b.astype(F32)).astype(BF16)

    side_high = side(add(high1, from_other))
    other_low = other(add(low2, from_side))
    low0, high0, grad0 = first((0,), rows, *args)
    own_low, own_high = middle((low0, side_low, other_low), (high0, side_high, other_high))

    low1, high2 = side(own_low), other(own_high)
    high1, low2 = side(own_high), other(own_low)
    low3, high3 = other(low1), side(high2)
    run = functools.partial(second, blocks=blocks, order=order, count=count, weight=weight,
                            w_gate=w_gate, w_up=w_up, w_down=w_down, tile=tile)
    dg, rows0 = run((0,), (), halves=(own_low, own_high), grad=grad0, done=(), prev=None)
    dg, rows12 = run((1, 2), (), halves=(low1, high1, low2, high2), grad=grad12, done=(), prev=dg)
    dg, keep, send = run((3,), ((0,), (1, 2)), halves=(low3, high3), grad=grad3,
                         done=(rows0, rows12), prev=dg)

    got = xor_permute(send, "expert", 1)
    total = keep[0] + got[0].astype(F32)
    for j in range(1, blocks // 2):
        piece = (keep[j] + got[j].astype(F32)).astype(BF16)
        total = total + xor_permute(piece, "expert", 2 * j).astype(F32)
    total = total.astype(BF16)
    return total[0], total[1], dg


def small(tokens, cotangent, expert_ids, route_weight, w_gate, w_up, w_down):
    blocks, slabs = lax.axis_size("expert"), lax.axis_size("tensor")
    local = w_gate.shape[0]
    experts = local * blocks
    length, top = expert_ids.shape
    capacity = 2 * length * top // experts
    most = 2 * capacity * blocks
    fewer = most * 3 // 4

    own = pack(tokens, cotangent, expert_ids, route_weight)
    even = [own] + [xor_permute(own, "expert", j) for j in range(2, blocks, 2)]
    odd = [xor_permute(v, "expert", 1) for v in even]
    parts = [v for both in zip(even, odd) for v in both]
    where = jnp.stack([lax.axis_index("expert"), lax.axis_index("tensor")]).astype(jnp.int32)
    order, fits, count, weight = route(parts, where, top, experts, local, slabs, fewer)
    run = [
        functools.partial(exchange, rows, blocks, order, count, weight, parts, w_gate, w_up, w_down)
        for rows in (fewer, most)
    ]
    return lax.cond(fits[0] > 0, *run)


def large(tokens, cotangent, expert_ids, route_weight, w_gate, w_up, w_down):
    resident_specialists = w_gate.shape[0]
    experts = resident_specialists * lax.axis_size("expert")
    tok_count = expert_ids.shape[0]
    top_count = expert_ids.shape[1]
    capacity = 2 * tok_count * top_count // experts
    model_width = tokens.shape[1]
    flat_ids = expert_ids.reshape(-1)
    onehot = (flat_ids[:, None] == jnp.arange(experts, dtype=jnp.int32)[None, :]).astype(jnp.int32)
    before = jnp.cumsum(onehot, axis=0) - onehot
    slot_index = jnp.sum(before * onehot, axis=1)
    target = flat_ids * capacity + slot_index
    chosen = (target[:, None] == jnp.arange(experts * capacity, dtype=jnp.int32)[None, :]).astype(F32)
    chosen = chosen.reshape(tok_count, top_count, experts * capacity)
    expert_assignment = jnp.sum(chosen, axis=1)
    weighted = jnp.sum(chosen * route_weight[:, :, None], axis=1)
    token_send = jnp.dot(expert_assignment.T.astype(BF16), tokens, preferred_element_type=F32)
    token_send = token_send.astype(BF16).reshape(experts, capacity, model_width)
    gradient_outgoing = jnp.dot(
        weighted.T, cotangent, precision=lax.Precision.HIGHEST, preferred_element_type=F32
    )
    gradient_outgoing = gradient_outgoing.astype(BF16).reshape(experts, capacity, model_width)
    token_rows = lax.all_to_all(token_send, "expert", split_axis=0, concat_axis=1, tiled=True)
    grad_rows = lax.all_to_all(gradient_outgoing, "expert", split_axis=0, concat_axis=1, tiled=True)
    pre_gate = jnp.einsum("erd,edf->erf", token_rows, w_gate, preferred_element_type=F32)
    pre_up = jnp.einsum("erd,edf->erf", token_rows, w_up, preferred_element_type=F32)
    slice_breadth = w_gate.shape[2] // lax.axis_size("tensor")
    gate_sum = lax.psum(pre_gate.astype(BF16), "tensor").astype(F32)
    up_sum = lax.psum(pre_up.astype(BF16), "tensor").astype(F32)
    sigmoid_all = jax.nn.sigmoid(gate_sum)
    hidden = (gate_sum * sigmoid_all * up_sum).astype(BF16)
    out_rows = jnp.einsum("erf,efd->erd", hidden, w_down, preferred_element_type=F32).astype(BF16)
    down_grad = jnp.einsum("erf,erd->efd", hidden, grad_rows, preferred_element_type=F32)
    offset = lax.axis_index("tensor") * slice_breadth
    gate_part = lax.dynamic_slice_in_dim(gate_sum, offset, slice_breadth, 2)
    up_part = lax.dynamic_slice_in_dim(up_sum, offset, slice_breadth, 2)
    sigmoid_part = lax.dynamic_slice_in_dim(sigmoid_all, offset, slice_breadth, 2)
    hidden_term = jnp.einsum("erd,efd->erf", grad_rows, w_down, preferred_element_type=F32)
    hidden_grad = lax.psum_scatter(
        hidden_term.astype(BF16), "tensor", scatter_dimension=2, tiled=True
    ).astype(F32)
    gate_grad = (
        hidden_grad * up_part * sigmoid_part * (1.0 + gate_part * (1.0 - sigmoid_part))
    ).astype(BF16)
    up_grad = (hidden_grad * gate_part * sigmoid_part).astype(BF16)
    gate_piece = lax.all_gather(gate_grad, "tensor", axis=2, tiled=True)
    up_piece = lax.all_gather(up_grad, "tensor", axis=2, tiled=True)
    running = jnp.einsum("erf,edf->erd", gate_piece, w_gate, preferred_element_type=F32)
    input_rows = running + jnp.einsum("erf,edf->erd", up_piece, w_up, preferred_element_type=F32)
    input_rows = input_rows.astype(BF16)
    returned_out = lax.all_to_all(out_rows, "expert", split_axis=1, concat_axis=0, tiled=True)
    returned_in = lax.all_to_all(input_rows, "expert", split_axis=1, concat_axis=0, tiled=True)
    returned_out = returned_out.reshape(experts * capacity, model_width)
    returned_in = returned_in.reshape(experts * capacity, model_width)
    mixed_out = jnp.dot(
        weighted, returned_out, precision=lax.Precision.HIGHEST, preferred_element_type=F32
    )
    input_grad = jnp.dot(expert_assignment.astype(BF16), returned_in, preferred_element_type=F32)
    return mixed_out.astype(BF16), input_grad.astype(BF16), down_grad.astype(BF16)


def local(tokens, cotangent, expert_ids, route_weight, w_gate, w_up, w_down):
    blocks, slabs = lax.axis_size("expert"), lax.axis_size("tensor")
    pairs = w_gate.shape[0] == 2 * slabs and slabs == 4
    few = blocks <= 8 and blocks & (blocks - 1) == 0
    body = small if pairs and few else large
    return body(tokens, cotangent, expert_ids, route_weight, w_gate, w_up, w_down)


def solution(mesh):
    return jax.shard_map(
        local,
        mesh=mesh,
        in_specs=(
            P("expert", "tensor"),
            P("expert", "tensor"),
            P("expert", None),
            P("expert", None),
            P("expert", "tensor", None),
            P("expert", "tensor", None),
            P("expert", None, "tensor"),
        ),
        out_specs=(P("expert", "tensor"), P("expert", "tensor"), P("expert", None, "tensor")),
        check_vma=False,
    )
```

```python
import functools
import jax
import jax.numpy as jnp
from jax import lax
from jax.experimental import pallas as pl
from jax.experimental.pallas import tpu as pltpu
from jax.sharding import PartitionSpec as P

BF16 = jnp.bfloat16
F32 = jnp.float32
VMEM_LIMIT = 63 << 20
META = 128
AHEAD = 3


def xor_permute(x, axis, mask):
    return lax.ppermute(x, axis, [(i, i ^ mask) for i in range(lax.axis_size(axis))])


def dot(a, b, contract):
    return lax.dot_general(a, b, ((contract[0], contract[1]), ((), ())), preferred_element_type=F32)


def whole(shape):
    return pl.BlockSpec(shape, lambda *_: (0,) * len(shape))


def pack_kernel(tokens_ref, grad_ref, ids_ref, weight_ref, out_ref):
    length, width = tokens_ref.shape
    out_ref[:, :width] = tokens_ref[...]
    out_ref[:, width : 2 * width] = grad_ref[...]
    weight = weight_ref[...]
    high = weight.astype(BF16).astype(F32)
    mid = (weight - high).astype(BF16).astype(F32)
    low = weight - high - mid
    fields = jnp.concatenate([ids_ref[...].astype(F32), high, mid, low], axis=0)
    if fields.shape[0] < length:
        fields = jnp.concatenate([fields, jnp.zeros((length - fields.shape[0], length), F32)], axis=0)
    fields = jnp.concatenate([fields, jnp.zeros((length, META - length), F32)], axis=1)
    out_ref[:, 2 * width :] = fields.astype(BF16)


def pack(tokens, cotangent, expert_ids, route_weight):
    length, width = tokens.shape
    return pl.pallas_call(
        pack_kernel,
        out_shape=jax.ShapeDtypeStruct((length, 2 * width + META), BF16),
        name="pack",
    )(tokens, cotangent, expert_ids.T, route_weight.T)


def route_kernel(blocks, top, experts, local, slabs, cap, *refs):
    metas, (order_ref, fits_ref, count_ref, weight_ref) = refs[:blocks], refs[blocks:]
    my_expert, my_slab = lax.axis_index("expert"), lax.axis_index("tensor")
    turned = jnp.concatenate([m[:, : m.shape[0]].astype(F32) for m in metas], axis=1)
    tokens = turned.shape[1]
    ids = turned[:top]
    weights = turned[top : 2 * top] + turned[2 * top : 3 * top] + turned[3 * top : 4 * top]

    all_names = lax.broadcasted_iota(jnp.int32, (experts, 1), 0).astype(F32)
    picked = jnp.zeros((experts, tokens), F32)
    for k in range(top):
        picked += (ids[k : k + 1] == all_names).astype(F32)
    down = jnp.sum(picked, axis=1, keepdims=True)
    across = dot(jnp.ones((8, tokens), BF16), picked.astype(BF16), ((1,), (1,)))[:1]
    row = lax.broadcasted_iota(jnp.int32, (experts, experts), 0)
    col = lax.broadcasted_iota(jnp.int32, (experts, experts), 1)
    same = row // local == col // local
    col_first = (across > down) | ((across == down) & (col < row))
    row_first = (down > across) | ((down == across) & (row < col))
    rank_down = jnp.sum((same & col_first).astype(F32), axis=1, keepdims=True)
    rank_across = jnp.sum((same & row_first).astype(F32), axis=0, keepdims=True)
    mate = same & (rank_across == (local - 1) - rank_down)
    pair = down + jnp.sum(jnp.where(mate, across, 0.0), axis=1, keepdims=True)
    fits_ref[0] = (jnp.max(pair) <= cap).astype(jnp.int32)

    names = (lax.broadcasted_iota(jnp.int32, (local, 1), 0) + my_expert * local).astype(F32)
    mine = jnp.zeros((local, tokens), F32)
    share = jnp.zeros((local, tokens), F32)
    for k in range(top):
        hit = ids[k : k + 1] == names
        mine += hit.astype(F32)
        share += jnp.where(hit, weights[k : k + 1], 0.0)
    earlier = (
        lax.broadcasted_iota(jnp.int32, (tokens, tokens), 0)
        < lax.broadcasted_iota(jnp.int32, (tokens, tokens), 1)
    ).astype(BF16)
    count = dot(mine.astype(BF16), earlier, ((1,), (0,)))
    count = jnp.where(mine > 0, count, -1.0)
    load = jnp.sum(mine, axis=1, keepdims=True)
    load_across = dot(jnp.ones((8, tokens), BF16), mine.astype(BF16), ((1,), (1,)))[:1]
    row = lax.broadcasted_iota(jnp.int32, (local, local), 0)
    col = lax.broadcasted_iota(jnp.int32, (local, local), 1)
    first = (load_across > load) | ((load_across == load) & (col < row))
    rank = jnp.sum(first.astype(F32), axis=1, keepdims=True)
    index = lax.broadcasted_iota(jnp.int32, (local, 1), 0).astype(F32)
    for place in range(slabs):
        slab = place ^ my_slab
        for end in range(2):
            wanted = (slab if end == 0 else local - 1 - slab).astype(F32)
            chosen = rank == wanted
            at = 2 * place + end
            order_ref[at] = jnp.sum(jnp.where(chosen, index, 0.0)).astype(jnp.int32)
            count_ref[at : at + 1] = jnp.sum(jnp.where(chosen, count, 0.0), axis=0, keepdims=True)
            weight_ref[at : at + 1] = jnp.sum(jnp.where(chosen, share, 0.0), axis=0, keepdims=True)


def route(parts, top, experts, local, slabs, cap):
    length, lanes = parts[0].shape
    tokens = length * len(parts)
    smem = pl.BlockSpec(memory_space=pltpu.SMEM)
    meta = pl.BlockSpec((length, META), lambda i: (0, lanes // META - 1))
    return pl.pallas_call(
        functools.partial(route_kernel, len(parts), top, experts, local, slabs, cap),
        grid=(1,),
        in_specs=[meta] * len(parts),
        out_specs=(smem, smem, whole((local, tokens)), whole((local, tokens))),
        compiler_params=pltpu.CompilerParams(vmem_limit_bytes=VMEM_LIMIT),
        out_shape=(
            jax.ShapeDtypeStruct((local,), jnp.int32),
            jax.ShapeDtypeStruct((1,), jnp.int32),
            jax.ShapeDtypeStruct((local, tokens), F32),
            jax.ShapeDtypeStruct((local, tokens), F32),
        ),
        name="route",
    )(*parts)


def picks(count_ref, at, end, rows):
    count = count_ref[pl.ds(at, 1), :]
    target = jnp.where(end == 0, count, jnp.where(count >= 0, (rows - 1) - count, -1.0))
    line = lax.broadcasted_iota(jnp.int32, (rows, count.shape[1]), 0).astype(F32)
    return line == target


ANY = pl.BlockSpec(memory_space=pl.ANY)
SMEM = pl.BlockSpec(memory_space=pltpu.SMEM)


def start(copies):
    for copy in copies:
        copy.start()


def first_kernel(places, blocks, order, count_hbm, weight_hbm, *refs):
    parts, refs = refs[:blocks], refs[blocks:]
    (gate_hbm, up_hbm, down_hbm), refs = refs[:3], refs[3:]
    halves, refs = refs[: 2 * len(places)], refs[2 * len(places) :]
    grad_out, refs = refs[0], refs[1:]
    (count_ref, weight_ref, data, gates, ups, downs, rows_ref, acc, sums, grads) = refs[:10]
    data_sem, weight_sem, out_sem = refs[10:]
    length = parts[0].shape[0]
    experts, rows, width = grads.shape
    half = rows // 2
    cut = downs.shape[1] // 2

    small_copies = [
        pltpu.make_async_copy(count_hbm, count_ref, data_sem.at[blocks]),
        pltpu.make_async_copy(weight_hbm, weight_ref, data_sem.at[blocks + 1]),
    ] + [
        pltpu.make_async_copy(
            parts[j].at[:, : 2 * width], data.at[j * length : (j + 1) * length, :], data_sem.at[j]
        )
        for j in range(blocks)
    ]

    def read(k, turn, expert):
        i, c = turn // 2, turn % 2
        part = pl.ds(pl.multiple_of(cut * c, cut), cut)
        source, held = ((gate_hbm, gates), (up_hbm, ups), (down_hbm, downs))[k]
        where = (part, slice(None)) if k == 2 else (slice(None), part)
        return pltpu.make_async_copy(
            source.at[(expert, *where)], held.at[(i, *where)], weight_sem.at[k, turn]
        )

    def ahead(k, turn, count):
        turn, k = turn + (k + count) // 3, (k + count) % 3

        @pl.when(turn < 2 * experts)
        def _():
            i = turn // 2
            read(k, turn, order[2 * nth(places, i // 2) + i % 2]).start()

    start(small_copies)
    for k in range(AHEAD):
        ahead(0, jnp.int32(0), k)
    for copy in small_copies:
        copy.wait()

    def body(turn, carry):
        i, c = turn // 2, turn % 2
        which, end = i // 2, i % 2
        lanes = pl.ds(pl.multiple_of(cut * c, cut), cut)

        @pl.when(c == 0)
        def _():
            at = 2 * nth(places, which) + end
            chosen = picks(count_ref, at, end, rows)
            select = chosen.astype(BF16)
            scale = jnp.sum(
                jnp.where(chosen, weight_ref[pl.ds(at, 1), :], 0.0), axis=1, keepdims=True
            )
            rows_ref[...] = dot(select, data[:, :width], ((1,), (0,))).astype(BF16)
            grads[i] = (dot(select, data[:, width:], ((1,), (0,))) * scale).astype(BF16)

        for k in range(3):
            read(k, turn, 0).wait()
            ahead(k, turn, AHEAD)
            if k < 2:
                value = dot(rows_ref[...], (gates, ups)[k][i, :, lanes], ((1,), (0,)))
            else:
                value = dot(grads[i], downs[i, lanes], ((1,), (1,)))

            @pl.when(end == 0)
            def _():
                acc[k, :, lanes] = value

            @pl.when(end == 1)
            def _():
                total = (acc[k, :, lanes] + value).astype(BF16)
                sums[2 * which, k, :, lanes] = total[:half]
                sums[2 * which + 1, k, :, lanes] = total[half:]

        for p in range(len(places)):

            @pl.when(turn == 4 * p + 3)
            def _():
                for h in range(2):
                    q = 2 * p + h
                    pltpu.make_async_copy(sums.at[q], halves[q], out_sem.at[q]).start()

        return carry

    lax.fori_loop(0, 2 * experts, body, 0)
    last = pltpu.make_async_copy(grads, grad_out, out_sem.at[2 * len(places)])
    last.start()
    for q in range(2 * len(places)):
        pltpu.make_async_copy(sums.at[q], halves[q], out_sem.at[q]).wait()
    last.wait()


def nth(places, which):
    value = places[0]
    for at in range(1, len(places)):
        value = jnp.where(which == at, places[at], value)
    return value


def first(places, rows, order, count, weight, parts, w_gate, w_up, w_down):
    _, width, hidden = w_gate.shape
    tokens = count.shape[1]
    experts = 2 * len(places)
    half = jax.ShapeDtypeStruct((3, rows // 2, hidden), BF16)
    return pl.pallas_call(
        functools.partial(first_kernel, places, len(parts)),
        in_specs=[SMEM] + [ANY] * (5 + len(parts)),
        out_specs=[ANY] * (experts + 1),
        scratch_shapes=[
            pltpu.VMEM(count.shape, F32),
            pltpu.VMEM(weight.shape, F32),
            pltpu.VMEM((tokens, 2 * width), BF16),
            pltpu.VMEM((experts, width, hidden), BF16),
            pltpu.VMEM((experts, width, hidden), BF16),
            pltpu.VMEM((experts, hidden, width), BF16),
            pltpu.VMEM((rows, width), BF16),
            pltpu.VMEM((3, rows, hidden), F32),
            pltpu.VMEM((experts, 3, rows // 2, hidden), BF16),
            pltpu.VMEM((experts, rows, width), BF16),
            pltpu.SemaphoreType.DMA((len(parts) + 2,)),
            pltpu.SemaphoreType.DMA((3, 2 * experts)),
            pltpu.SemaphoreType.DMA((experts + 1,)),
        ],
        out_shape=[half] * experts + [jax.ShapeDtypeStruct((experts, rows, width), BF16)],
        compiler_params=pltpu.CompilerParams(vmem_limit_bytes=VMEM_LIMIT),
        cost_estimate=pl.CostEstimate(
            flops=6 * experts * rows * width * hidden,
            bytes_accessed=6 * experts * width * hidden,
            transcendentals=0,
        ),
        name="first" + "".join(map(str, places)),
    )(order, count, weight, *parts, w_gate, w_up, w_down)


def join_kernel(a_ref, b_ref, c_ref, d_ref, first_ref, second_ref):
    first_ref[...] = (a_ref[...].astype(F32) + b_ref[...].astype(F32)).astype(BF16)
    second_ref[...] = (c_ref[...].astype(F32) + d_ref[...].astype(F32)).astype(BF16)


def join(a, b, c, d):
    shape = jax.ShapeDtypeStruct(a.shape, a.dtype)
    return pl.pallas_call(
        join_kernel,
        grid=(1,),
        in_specs=[whole(a.shape)] * 4,
        out_specs=[whole(a.shape)] * 2,
        out_shape=(shape, shape),
        compiler_params=pltpu.CompilerParams(vmem_limit_bytes=VMEM_LIMIT),
        cost_estimate=pl.CostEstimate(flops=2 * a.size, bytes_accessed=12 * a.size, transcendentals=0),
        name="join",
    )(a, b, c, d)


def middle_kernel(*refs):
    sources, outs = refs[:6], refs[6:]
    for h in range(2):
        own, side, other = sources[3 * h : 3 * h + 3]
        gate, up, grad = [
            own[i].astype(F32) + side[i].astype(F32) + other[i].astype(F32) for i in range(3)
        ]
        sig = jax.nn.sigmoid(gate)
        outs[h][0] = (gate * sig * up).astype(BF16)
        outs[h][1] = (grad * up * sig * (1.0 + gate * (1.0 - sig))).astype(BF16)
        outs[h][2] = (grad * gate * sig).astype(BF16)


def middle(low, high):
    _, half, hidden = low[0].shape
    tile = hidden // 3
    spec = pl.BlockSpec((3, half, tile), lambda f: (0, 0, f))
    shape = jax.ShapeDtypeStruct((3, half, hidden), BF16)
    return pl.pallas_call(
        middle_kernel,
        grid=(hidden // tile,),
        in_specs=[spec] * 6,
        out_specs=(spec, spec),
        out_shape=(shape, shape),
        compiler_params=pltpu.CompilerParams(vmem_limit_bytes=VMEM_LIMIT),
        cost_estimate=pl.CostEstimate(
            flops=40 * half * hidden, bytes_accessed=48 * half * hidden, transcendentals=2 * half * hidden
        ),
        name="middle",
    )(*low, *high)


def second_kernel(places, has_prev, last, order, count_hbm, weight_hbm, *refs):
    halves, refs = refs[: 2 * len(places)], refs[2 * len(places) :]
    (grad_hbm, gate_hbm, up_hbm, down_hbm), refs = refs[:4], refs[4:]
    done_hbm, refs = refs[: len(last)], refs[len(last) :]
    refs = refs[1:] if has_prev else refs
    dg_hbm, refs = refs[0], refs[1:]
    outs, refs = (refs[:2], refs[2:]) if last else (refs[:1], refs[1:])
    (count_ref, weight_ref, work, grads, gates, ups, downs, out_acc, in_acc, rows_ref, stage), refs = (
        refs[:11],
        refs[11:],
    )
    if last:
        (keep_ref, send_ref, high, low, plain, total), refs = refs[:6], refs[6:]
        done, refs = refs[: len(last)], refs[len(last) :]
    data_sem, weight_sem, out_sem = refs
    rows, hidden = work.shape[2], work.shape[3]
    half, cut = rows // 2, hidden // 2
    experts = grads.shape[0]

    data_copies = [
        pltpu.make_async_copy(count_hbm, count_ref, data_sem.at[0]),
        pltpu.make_async_copy(weight_hbm, weight_ref, data_sem.at[1]),
        pltpu.make_async_copy(grad_hbm, grads, data_sem.at[2]),
    ]
    for q in range(2 * len(places)):
        data_copies.append(
            pltpu.make_async_copy(
                halves[q], work.at[q // 2, :, pl.ds(half * (q % 2), half)], data_sem.at[3 + q]
            )
        )
    done_copies = []
    for q in range(len(last)):
        done_copies.append(
            pltpu.make_async_copy(done_hbm[q], done[q], data_sem.at[3 + 2 * len(places) + q])
        )

    def read(k, turn, expert):
        i, c = turn // 2, turn % 2
        part = pl.ds(pl.multiple_of(cut * c, cut), cut)
        source, held = ((down_hbm, downs), (gate_hbm, gates), (up_hbm, ups))[k]
        where = (part, slice(None)) if k == 0 else (slice(None), part)
        return pltpu.make_async_copy(
            source.at[(expert, *where)], held.at[(i, *where)], weight_sem.at[k, turn]
        )

    def expert_of(turn):
        i = turn // 2
        return order[2 * nth(places, i // 2) + i % 2]

    def ahead(k, turn, count):
        turn, k = turn + (k + count) // 3, (k + count) % 3

        @pl.when(turn < 2 * experts)
        def _():
            read(k, turn, expert_of(turn)).start()

    def writes(c, expert):
        return pltpu.make_async_copy(
            stage.at[c], dg_hbm.at[expert, pl.ds(pl.multiple_of(cut * c, cut), cut)], out_sem.at[c]
        )

    start(data_copies)
    for k in range(AHEAD):
        ahead(0, jnp.int32(0), k)
    start(done_copies)
    for copy in data_copies:
        copy.wait()

    if last:
        order_of = [p for group in last for p in group] + list(places)
        for slot, place in enumerate(order_of):
            scale, seen = 0.0, 0.0
            for e in range(2):
                at = 2 * place + e
                chosen = picks(count_ref, at, e, rows)
                scale = scale + jnp.where(chosen, weight_ref[at : at + 1, :], 0.0)
                seen = seen + chosen.astype(F32)
            part = scale.astype(BF16)
            high[slot] = part
            low[slot] = (scale - part.astype(F32)).astype(BF16)
            plain[slot] = seen.astype(BF16)

    def add(slot, out_rows, in_rows):
        out = dot(high[slot], out_rows, ((0,), (0,))) + dot(low[slot], out_rows, ((0,), (0,)))
        return out, dot(plain[slot], in_rows, ((0,), (0,)))

    def body(turn, carry):
        i, c = turn // 2, turn % 2
        which, end = i // 2, i % 2
        lanes = pl.ds(pl.multiple_of(cut * c, cut), cut)
        read(0, turn, 0).wait()
        ahead(0, turn, AHEAD)

        @pl.when(turn >= 2)
        def _():
            writes(c, 0).wait()

        stage[c] = dot(work[which, 0, :, lanes], grads[i], ((0,), (0,))).astype(BF16)
        writes(c, expert_of(turn)).start()
        out_part = dot(work[which, 0, :, lanes], downs[i, lanes], ((1,), (0,)))

        @pl.when(c == 0)
        def _():
            out_acc[...] = out_part
            in_acc[...] = jnp.zeros_like(in_acc)

        @pl.when(c == 1)
        def _():
            out_acc[...] += out_part

        for k in range(1, 3):
            read(k, turn, 0).wait()
            ahead(k, turn, AHEAD)
            in_acc[...] += dot(
                work[which, k, :, lanes], (gates, ups)[k - 1][i, :, lanes], ((1,), (1,))
            )

        @pl.when((c == 1) & (end == 0))
        def _():
            rows_ref[which, 0] = out_acc[...].astype(BF16)
            rows_ref[which, 1] = in_acc[...].astype(BF16)

        @pl.when((c == 1) & (end == 1))
        def _():
            at = 2 * nth(places, which) + 1
            own = jnp.max(picks(count_ref, at, 1, rows).astype(F32), axis=1, keepdims=True) > 0
            for k, value in enumerate((out_acc, in_acc)):
                before = rows_ref[which, k].astype(F32)
                rows_ref[which, k] = jnp.where(own, value[...], before).astype(BF16)

        if last:

            @pl.when(turn == 1)
            def _():
                for copy in done_copies:
                    copy.wait()
                slot = 0
                for d, group in zip(done, last):
                    for g in range(len(group)):
                        for k, value in enumerate(add(slot, d[g, 0], d[g, 1])):
                            total[k] = value if slot == 0 else total[k] + value
                        slot += 1

        return carry

    lax.fori_loop(0, 2 * experts, body, 0)
    if last:
        length = keep_ref.shape[2]
        for k, value in enumerate(add(len(order_of) - 1, rows_ref[0, 0], rows_ref[0, 1])):
            value = total[k] + value
            for j in range(keep_ref.shape[0]):
                keep_ref[j, k] = value[2 * j * length : (2 * j + 1) * length]
                send_ref[j, k] = value[(2 * j + 1) * length : (2 * j + 2) * length].astype(BF16)
        finals = [
            pltpu.make_async_copy(send_ref, outs[1], out_sem.at[3]),
            pltpu.make_async_copy(keep_ref, outs[0], out_sem.at[2]),
        ]
    else:
        finals = [pltpu.make_async_copy(rows_ref, outs[0], out_sem.at[2])]
    start(finals)
    for c in range(2):
        writes(c, 0).wait()
    for copy in finals:
        copy.wait()


def second(places, last, blocks, order, count, weight, halves, grad, w_gate, w_up, w_down, done, prev):
    local, width, hidden = w_gate.shape
    tokens = count.shape[1]
    rows = grad.shape[1]
    experts = 2 * len(places)
    operands = [order, count, weight, *halves, grad, w_gate, w_up, w_down, *done]
    aliases = {}
    if prev is not None:
        operands.append(prev)
        aliases = {len(operands) - 1: 0}
    row_shape = (len(places), 2, rows, width)
    scratch = [
        pltpu.VMEM(count.shape, F32),
        pltpu.VMEM(weight.shape, F32),
        pltpu.VMEM((len(places), 3, rows, hidden), BF16),
        pltpu.VMEM(grad.shape, BF16),
        pltpu.VMEM((experts, width, hidden), BF16),
        pltpu.VMEM((experts, width, hidden), BF16),
        pltpu.VMEM((experts, hidden, width), BF16),
        pltpu.VMEM((rows, width), F32),
        pltpu.VMEM((rows, width), F32),
        pltpu.VMEM(row_shape, BF16),
        pltpu.VMEM((2, hidden // 2, width), BF16),
    ]
    outs = [jax.ShapeDtypeStruct((local, hidden, width), BF16)]
    if last:
        shape = (blocks // 2, 2, tokens // blocks, width)
        outs += [jax.ShapeDtypeStruct(shape, F32), jax.ShapeDtypeStruct(shape, BF16)]
        scratch += [pltpu.VMEM(shape, F32), pltpu.VMEM(shape, BF16)]
        scratch += [pltpu.VMEM((local // 2, rows, tokens), BF16)] * 3
        scratch += [pltpu.VMEM((2, tokens, width), F32)]
        scratch += [pltpu.VMEM(d.shape, BF16) for d in done]
    else:
        outs += [jax.ShapeDtypeStruct(row_shape, BF16)]
    scratch += [
        pltpu.SemaphoreType.DMA((3 + experts + len(done),)),
        pltpu.SemaphoreType.DMA((3, 2 * experts)),
        pltpu.SemaphoreType.DMA((4,)),
    ]
    return pl.pallas_call(
        functools.partial(second_kernel, places, prev is not None, last),
        in_specs=[SMEM] + [ANY] * (len(operands) - 1),
        out_specs=[ANY] * len(outs),
        scratch_shapes=scratch,
        out_shape=outs,
        input_output_aliases=aliases,
        compiler_params=pltpu.CompilerParams(vmem_limit_bytes=VMEM_LIMIT),
        cost_estimate=pl.CostEstimate(
            flops=8 * experts * rows * width * hidden,
            bytes_accessed=8 * experts * width * hidden,
            transcendentals=0,
        ),
        name="second" + "".join(map(str, places)),
    )(*operands)


def exchange(rows, blocks, order, count, weight, parts, w_gate, w_up, w_down):
    args = (order, count, weight, parts, w_gate, w_up, w_down)
    side = functools.partial(xor_permute, axis="tensor", mask=1)
    other = functools.partial(xor_permute, axis="tensor", mask=2)

    low3, high3, grad3 = first((3,), rows, *args)
    from_side, from_other = side(low3), other(high3)
    low1, high1, low2, high2, grad12 = first((1, 2), rows, *args)
    side_low, other_high = side(low1), other(high2)

    joined_high, joined_low = join(high1, from_other, low2, from_side)
    side_high, other_low = side(joined_high), other(joined_low)
    low0, high0, grad0 = first((0,), rows, *args)
    own_low, own_high = middle((low0, side_low, other_low), (high0, side_high, other_high))

    low1, high2 = side(own_low), other(own_high)
    high1, low2 = side(own_high), other(own_low)
    low3, high3 = other(low1), side(high2)
    run = functools.partial(second, blocks=blocks, order=order, count=count, weight=weight,
                            w_gate=w_gate, w_up=w_up, w_down=w_down)
    dg, rows0 = run((0,), (), halves=(own_low, own_high), grad=grad0, done=(), prev=None)
    dg, rows12 = run((1, 2), (), halves=(low1, high1, low2, high2), grad=grad12, done=(), prev=dg)
    dg, keep, send = run((3,), ((0,), (1, 2)), halves=(low3, high3), grad=grad3,
                         done=(rows0, rows12), prev=dg)

    got = xor_permute(send, "expert", 1)
    total = keep[0] + got[0].astype(F32)
    for j in range(1, blocks // 2):
        piece = (keep[j] + got[j].astype(F32)).astype(BF16)
        total = total + xor_permute(piece, "expert", 2 * j).astype(F32)
    total = total.astype(BF16)
    return total[0], total[1], dg


def small(tokens, cotangent, expert_ids, route_weight, w_gate, w_up, w_down):
    blocks, slabs = lax.axis_size("expert"), lax.axis_size("tensor")
    local = w_gate.shape[0]
    experts = local * blocks
    length, top = expert_ids.shape
    capacity = 2 * length * top // experts
    most = 2 * capacity * blocks
    fewer = most * 3 // 4

    own = pack(tokens, cotangent, expert_ids, route_weight)
    even = [own] + [xor_permute(own, "expert", j) for j in range(2, blocks, 2)]
    odd = [xor_permute(v, "expert", 1) for v in even]
    parts = [v for both in zip(even, odd) for v in both]
    order, fits, count, weight = route(parts, top, experts, local, slabs, fewer)
    run = [
        functools.partial(exchange, rows, blocks, order, count, weight, parts, w_gate, w_up, w_down)
        for rows in (fewer, most)
    ]
    return lax.cond(fits[0] > 0, *run)


def large(tokens, cotangent, expert_ids, route_weight, w_gate, w_up, w_down):
    resident_specialists = w_gate.shape[0]
    experts = resident_specialists * lax.axis_size("expert")
    tok_count = expert_ids.shape[0]
    top_count = expert_ids.shape[1]
    capacity = 2 * tok_count * top_count // experts
    model_width = tokens.shape[1]
    flat_ids = expert_ids.reshape(-1)
    onehot = (flat_ids[:, None] == jnp.arange(experts, dtype=jnp.int32)[None, :]).astype(jnp.int32)
    before = jnp.cumsum(onehot, axis=0) - onehot
    slot_index = jnp.sum(before * onehot, axis=1)
    target = flat_ids * capacity + slot_index
    chosen = (target[:, None] == jnp.arange(experts * capacity, dtype=jnp.int32)[None, :]).astype(F32)
    chosen = chosen.reshape(tok_count, top_count, experts * capacity)
    expert_assignment = jnp.sum(chosen, axis=1)
    weighted = jnp.sum(chosen * route_weight[:, :, None], axis=1)
    token_send = jnp.dot(expert_assignment.T.astype(BF16), tokens, preferred_element_type=F32)
    token_send = token_send.astype(BF16).reshape(experts, capacity, model_width)
    gradient_outgoing = jnp.dot(
        weighted.T, cotangent, precision=lax.Precision.HIGHEST, preferred_element_type=F32
    )
    gradient_outgoing = gradient_outgoing.astype(BF16).reshape(experts, capacity, model_width)
    token_rows = lax.all_to_all(token_send, "expert", split_axis=0, concat_axis=1, tiled=True)
    grad_rows = lax.all_to_all(gradient_outgoing, "expert", split_axis=0, concat_axis=1, tiled=True)
    pre_gate = jnp.einsum("erd,edf->erf", token_rows, w_gate, preferred_element_type=F32)
    pre_up = jnp.einsum("erd,edf->erf", token_rows, w_up, preferred_element_type=F32)
    slice_breadth = w_gate.shape[2] // lax.axis_size("tensor")
    gate_sum = lax.psum(pre_gate.astype(BF16), "tensor").astype(F32)
    up_sum = lax.psum(pre_up.astype(BF16), "tensor").astype(F32)
    sigmoid_all = jax.nn.sigmoid(gate_sum)
    hidden = (gate_sum * sigmoid_all * up_sum).astype(BF16)
    out_rows = jnp.einsum("erf,efd->erd", hidden, w_down, preferred_element_type=F32).astype(BF16)
    down_grad = jnp.einsum("erf,erd->efd", hidden, grad_rows, preferred_element_type=F32)
    offset = lax.axis_index("tensor") * slice_breadth
    gate_part = lax.dynamic_slice_in_dim(gate_sum, offset, slice_breadth, 2)
    up_part = lax.dynamic_slice_in_dim(up_sum, offset, slice_breadth, 2)
    sigmoid_part = lax.dynamic_slice_in_dim(sigmoid_all, offset, slice_breadth, 2)
    hidden_term = jnp.einsum("erd,efd->erf", grad_rows, w_down, preferred_element_type=F32)
    hidden_grad = lax.psum_scatter(
        hidden_term.astype(BF16), "tensor", scatter_dimension=2, tiled=True
    ).astype(F32)
    gate_grad = (
        hidden_grad * up_part * sigmoid_part * (1.0 + gate_part * (1.0 - sigmoid_part))
    ).astype(BF16)
    up_grad = (hidden_grad * gate_part * sigmoid_part).astype(BF16)
    gate_piece = lax.all_gather(gate_grad, "tensor", axis=2, tiled=True)
    up_piece = lax.all_gather(up_grad, "tensor", axis=2, tiled=True)
    running = jnp.einsum("erf,edf->erd", gate_piece, w_gate, preferred_element_type=F32)
    input_rows = running + jnp.einsum("erf,edf->erd", up_piece, w_up, preferred_element_type=F32)
    input_rows = input_rows.astype(BF16)
    returned_out = lax.all_to_all(out_rows, "expert", split_axis=1, concat_axis=0, tiled=True)
    returned_in = lax.all_to_all(input_rows, "expert", split_axis=1, concat_axis=0, tiled=True)
    returned_out = returned_out.reshape(experts * capacity, model_width)
    returned_in = returned_in.reshape(experts * capacity, model_width)
    mixed_out = jnp.dot(
        weighted, returned_out, precision=lax.Precision.HIGHEST, preferred_element_type=F32
    )
    input_grad = jnp.dot(expert_assignment.astype(BF16), returned_in, preferred_element_type=F32)
    return mixed_out.astype(BF16), input_grad.astype(BF16), down_grad.astype(BF16)


def local(tokens, cotangent, expert_ids, route_weight, w_gate, w_up, w_down):
    blocks, slabs = lax.axis_size("expert"), lax.axis_size("tensor")
    pairs = w_gate.shape[0] == 2 * slabs and slabs == 4
    few = blocks <= 8 and blocks & (blocks - 1) == 0
    short = 4 * expert_ids.shape[1] <= expert_ids.shape[0] <= META
    body = small if pairs and few and short else large
    return body(tokens, cotangent, expert_ids, route_weight, w_gate, w_up, w_down)


def solution(mesh):
    return jax.shard_map(
        local,
        mesh=mesh,
        in_specs=(
            P("expert", "tensor"),
            P("expert", "tensor"),
            P("expert", None),
            P("expert", None),
            P("expert", "tensor", None),
            P("expert", "tensor", None),
            P("expert", None, "tensor"),
        ),
        out_specs=(P("expert", "tensor"), P("expert", "tensor"), P("expert", None, "tensor")),
        check_vma=False,
    )
```

```python
import functools
import jax
import jax.numpy as jnp
from jax import lax
from jax.experimental import pallas as pl
from jax.experimental.pallas import tpu as pltpu
from jax.sharding import PartitionSpec as P

BF16 = jnp.bfloat16
F32 = jnp.float32
VMEM_LIMIT = 63 << 20
META = 128
AHEAD = 3


def xor_permute(x, axis, mask):
    return lax.ppermute(x, axis, [(i, i ^ mask) for i in range(lax.axis_size(axis))])


def dot(a, b, contract):
    return lax.dot_general(a, b, ((contract[0], contract[1]), ((), ())), preferred_element_type=F32)


def whole(shape):
    return pl.BlockSpec(shape, lambda *_: (0,) * len(shape))


def pack_kernel(tokens_ref, grad_ref, ids_ref, weight_ref, out_ref):
    length, width = tokens_ref.shape
    out_ref[:, :width] = tokens_ref[...]
    out_ref[:, width : 2 * width] = grad_ref[...]
    weight = weight_ref[...]
    high = weight.astype(BF16).astype(F32)
    mid = (weight - high).astype(BF16).astype(F32)
    low = weight - high - mid
    fields = jnp.concatenate([ids_ref[...].astype(F32), high, mid, low], axis=0)
    if fields.shape[0] < length:
        fields = jnp.concatenate([fields, jnp.zeros((length - fields.shape[0], length), F32)], axis=0)
    fields = jnp.concatenate([fields, jnp.zeros((length, META - length), F32)], axis=1)
    out_ref[:, 2 * width :] = fields.astype(BF16)


def pack(tokens, cotangent, expert_ids, route_weight):
    length, width = tokens.shape
    return pl.pallas_call(
        pack_kernel,
        out_shape=jax.ShapeDtypeStruct((length, 2 * width + META), BF16),
        name="pack",
    )(tokens, cotangent, expert_ids.T, route_weight.T)


def route_kernel(blocks, top, experts, local, slabs, cap, *refs):
    metas, (order_ref, fits_ref, count_ref, weight_ref) = refs[:blocks], refs[blocks:]
    my_expert, my_slab = lax.axis_index("expert"), lax.axis_index("tensor")
    turned = jnp.concatenate([m[:, : m.shape[0]].astype(F32) for m in metas], axis=1)
    tokens = turned.shape[1]
    ids = turned[:top]
    weights = turned[top : 2 * top] + turned[2 * top : 3 * top] + turned[3 * top : 4 * top]

    all_names = lax.broadcasted_iota(jnp.int32, (experts, 1), 0).astype(F32)
    picked = jnp.zeros((experts, tokens), F32)
    for k in range(top):
        picked += (ids[k : k + 1] == all_names).astype(F32)
    down = jnp.sum(picked, axis=1, keepdims=True)
    across = dot(jnp.ones((8, tokens), BF16), picked.astype(BF16), ((1,), (1,)))[:1]
    row = lax.broadcasted_iota(jnp.int32, (experts, experts), 0)
    col = lax.broadcasted_iota(jnp.int32, (experts, experts), 1)
    same = row // local == col // local
    col_first = (across > down) | ((across == down) & (col < row))
    row_first = (down > across) | ((down == across) & (row < col))
    rank_down = jnp.sum((same & col_first).astype(F32), axis=1, keepdims=True)
    rank_across = jnp.sum((same & row_first).astype(F32), axis=0, keepdims=True)
    mate = same & (rank_across == (local - 1) - rank_down)
    pair = down + jnp.sum(jnp.where(mate, across, 0.0), axis=1, keepdims=True)
    fits_ref[0] = (jnp.max(pair) <= cap).astype(jnp.int32)

    names = (lax.broadcasted_iota(jnp.int32, (local, 1), 0) + my_expert * local).astype(F32)
    mine = jnp.zeros((local, tokens), F32)
    share = jnp.zeros((local, tokens), F32)
    for k in range(top):
        hit = ids[k : k + 1] == names
        mine += hit.astype(F32)
        share += jnp.where(hit, weights[k : k + 1], 0.0)
    earlier = (
        lax.broadcasted_iota(jnp.int32, (tokens, tokens), 0)
        < lax.broadcasted_iota(jnp.int32, (tokens, tokens), 1)
    ).astype(BF16)
    count = dot(mine.astype(BF16), earlier, ((1,), (0,)))
    count = jnp.where(mine > 0, count, -1.0)
    load = jnp.sum(mine, axis=1, keepdims=True)
    load_across = dot(jnp.ones((8, tokens), BF16), mine.astype(BF16), ((1,), (1,)))[:1]
    row = lax.broadcasted_iota(jnp.int32, (local, local), 0)
    col = lax.broadcasted_iota(jnp.int32, (local, local), 1)
    first = (load_across > load) | ((load_across == load) & (col < row))
    rank = jnp.sum(first.astype(F32), axis=1, keepdims=True)
    index = lax.broadcasted_iota(jnp.int32, (local, 1), 0).astype(F32)
    for place in range(slabs):
        slab = place ^ my_slab
        for end in range(2):
            wanted = (slab if end == 0 else local - 1 - slab).astype(F32)
            chosen = rank == wanted
            at = 2 * place + end
            order_ref[at] = jnp.sum(jnp.where(chosen, index, 0.0)).astype(jnp.int32)
            count_ref[at : at + 1] = jnp.sum(jnp.where(chosen, count, 0.0), axis=0, keepdims=True)
            weight_ref[at : at + 1] = jnp.sum(jnp.where(chosen, share, 0.0), axis=0, keepdims=True)


def route(parts, top, experts, local, slabs, cap):
    length, lanes = parts[0].shape
    tokens = length * len(parts)
    smem = pl.BlockSpec(memory_space=pltpu.SMEM)
    meta = pl.BlockSpec((length, META), lambda i: (0, lanes // META - 1))
    return pl.pallas_call(
        functools.partial(route_kernel, len(parts), top, experts, local, slabs, cap),
        grid=(1,),
        in_specs=[meta] * len(parts),
        out_specs=(smem, smem, whole((local, tokens)), whole((local, tokens))),
        compiler_params=pltpu.CompilerParams(vmem_limit_bytes=VMEM_LIMIT),
        out_shape=(
            jax.ShapeDtypeStruct((local,), jnp.int32),
            jax.ShapeDtypeStruct((1,), jnp.int32),
            jax.ShapeDtypeStruct((local, tokens), F32),
            jax.ShapeDtypeStruct((local, tokens), F32),
        ),
        name="route",
    )(*parts)


def picks(count_ref, at, end, rows):
    count = count_ref[pl.ds(at, 1), :]
    target = jnp.where(end == 0, count, jnp.where(count >= 0, (rows - 1) - count, -1.0))
    line = lax.broadcasted_iota(jnp.int32, (rows, count.shape[1]), 0).astype(F32)
    return line == target


ANY = pl.BlockSpec(memory_space=pl.ANY)
SMEM = pl.BlockSpec(memory_space=pltpu.SMEM)


def start(copies):
    for copy in copies:
        copy.start()


def first_kernel(places, blocks, order, count_hbm, weight_hbm, *refs):
    parts, refs = refs[:blocks], refs[blocks:]
    sources, refs = refs[:3], refs[3:]
    halves, refs = refs[: 2 * len(places)], refs[2 * len(places) :]
    grad_out, refs = refs[0], refs[1:]
    (count_ref, weight_ref, data, downs, gates, ups, rows_ref, turned_ref, sums, grads) = refs[:10]
    data_sem, weight_sem, out_sem = refs[10:]
    length = parts[0].shape[0]
    experts, rows, width = grads.shape
    half, cut = rows // 2, sums.shape[3] // 2

    small_copies = [
        pltpu.make_async_copy(count_hbm, count_ref, data_sem.at[blocks]),
        pltpu.make_async_copy(weight_hbm, weight_ref, data_sem.at[blocks + 1]),
    ] + [
        pltpu.make_async_copy(
            parts[j].at[:, : 2 * width], data.at[j * length : (j + 1) * length, :], data_sem.at[j]
        )
        for j in range(blocks)
    ]

    def read(k, end, which, expert):
        span = slice(width * end, width * (end + 1))
        if k == 0:
            held = downs.at[which, :, span]
        else:
            held = (gates, ups)[k - 1].at[which, span]
        return pltpu.make_async_copy(
            sources[k].at[expert], held, weight_sem.at[2 * k + end, which]
        )

    def ahead(turn, which):
        which, turn = which + turn // 6, turn % 6

        @pl.when(which < len(places))
        def _():
            end = turn % 2
            read(turn // 2, end, which, order[2 * nth(places, which) + end]).start()

    start(small_copies)
    for turn in range(AHEAD):
        ahead(turn, jnp.int32(0))
    for copy in small_copies:
        copy.wait()
    last = pltpu.make_async_copy(grads, grad_out, out_sem.at[2 * len(places)])

    def body(which, carry):
        at = 2 * nth(places, which)
        chosen = jnp.concatenate([picks(count_ref, at + e, e, rows) for e in range(2)], axis=0)
        share = jnp.concatenate(
            [jnp.broadcast_to(weight_ref[pl.ds(at + e, 1), :], chosen[:rows].shape) for e in range(2)],
            axis=0,
        )
        scale = jnp.sum(jnp.where(chosen, share, 0.0), axis=1, keepdims=True)
        select = chosen.astype(BF16)
        found = dot(select, data[:, :width], ((1,), (0,))).astype(BF16)
        back = (dot(select, data[:, width:], ((1,), (0,))) * scale).astype(BF16)
        for e in range(2):
            span = slice(width * e, width * (e + 1))
            rows_ref[:, span] = found[rows * e : rows * (e + 1)]
            turned_ref[:, span] = back[rows * e : rows * (e + 1)]
            grads[2 * which + e] = back[rows * e : rows * (e + 1)]

        @pl.when(which == len(places) - 1)
        def _():
            last.start()

        for k in range(3):
            for e in range(2):
                read(k, e, which, 0).wait()
                ahead(2 * k + e + AHEAD, which)

            def columns(c, carry):
                lanes = pl.ds(pl.multiple_of(cut * c, cut), cut)
                if k == 0:
                    value = dot(turned_ref[...], downs[which, lanes], ((1,), (1,)))
                else:
                    value = dot(rows_ref[...], (gates, ups)[k - 1][which, :, lanes], ((1,), (0,)))
                value = value.astype(BF16)
                for h in range(2):
                    sums[2 * which + h, (k + 2) % 3, :, lanes] = value[half * h : half * (h + 1)]
                return carry

            lax.fori_loop(0, 2, columns, 0)
            for p in range(len(places)):

                @pl.when(which == p)
                def _():
                    for h in range(2):
                        q, slot = 2 * p + h, (k + 2) % 3
                        pltpu.make_async_copy(
                            sums.at[q, slot], halves[q].at[slot], out_sem.at[q]
                        ).start()

        return carry

    lax.fori_loop(0, len(places), body, 0)
    for q in range(2 * len(places)):
        pltpu.make_async_copy(sums.at[q], halves[q], out_sem.at[q]).wait()
    last.wait()


def nth(places, which):
    value = places[0]
    for at in range(1, len(places)):
        value = jnp.where(which == at, places[at], value)
    return value


def first(places, rows, order, count, weight, parts, w_gate, w_up, w_down):
    _, width, hidden = w_gate.shape
    tokens = count.shape[1]
    experts = 2 * len(places)
    half = jax.ShapeDtypeStruct((3, rows // 2, hidden), BF16)
    return pl.pallas_call(
        functools.partial(first_kernel, places, len(parts)),
        in_specs=[SMEM] + [ANY] * (5 + len(parts)),
        out_specs=[ANY] * (experts + 1),
        scratch_shapes=[
            pltpu.VMEM(count.shape, F32),
            pltpu.VMEM(weight.shape, F32),
            pltpu.VMEM((tokens, 2 * width), BF16),
            pltpu.VMEM((len(places), hidden, 2 * width), BF16),
            pltpu.VMEM((len(places), 2 * width, hidden), BF16),
            pltpu.VMEM((len(places), 2 * width, hidden), BF16),
            pltpu.VMEM((rows, 2 * width), BF16),
            pltpu.VMEM((rows, 2 * width), BF16),
            pltpu.VMEM((experts, 3, rows // 2, hidden), BF16),
            pltpu.VMEM((experts, rows, width), BF16),
            pltpu.SemaphoreType.DMA((len(parts) + 2,)),
            pltpu.SemaphoreType.DMA((6, len(places))),
            pltpu.SemaphoreType.DMA((experts + 1,)),
        ],
        out_shape=[half] * experts + [jax.ShapeDtypeStruct((experts, rows, width), BF16)],
        compiler_params=pltpu.CompilerParams(vmem_limit_bytes=VMEM_LIMIT),
        cost_estimate=pl.CostEstimate(
            flops=6 * experts * rows * width * hidden,
            bytes_accessed=6 * experts * width * hidden,
            transcendentals=0,
        ),
        name="first" + "".join(map(str, places)),
    )(order, count, weight, *parts, w_down, w_gate, w_up)


def join_kernel(a_ref, b_ref, c_ref, d_ref, first_ref, second_ref):
    first_ref[...] = (a_ref[...].astype(F32) + b_ref[...].astype(F32)).astype(BF16)
    second_ref[...] = (c_ref[...].astype(F32) + d_ref[...].astype(F32)).astype(BF16)


def join(a, b, c, d):
    shape = jax.ShapeDtypeStruct(a.shape, a.dtype)
    return pl.pallas_call(
        join_kernel,
        grid=(1,),
        in_specs=[whole(a.shape)] * 4,
        out_specs=[whole(a.shape)] * 2,
        out_shape=(shape, shape),
        compiler_params=pltpu.CompilerParams(vmem_limit_bytes=VMEM_LIMIT),
        cost_estimate=pl.CostEstimate(flops=2 * a.size, bytes_accessed=12 * a.size, transcendentals=0),
        name="join",
    )(a, b, c, d)


def middle_kernel(*refs):
    sources, outs, (held, made, in_sem, out_sem) = refs[:6], refs[6:8], refs[8:]
    reads = [pltpu.make_async_copy(sources[q], held.at[q], in_sem.at[q]) for q in range(6)]
    writes = [pltpu.make_async_copy(made.at[h], outs[h], out_sem.at[h]) for h in range(2)]
    start(reads)
    for h in range(2):
        for q in range(3 * h, 3 * h + 3):
            reads[q].wait()
        gate, up, grad = [
            held[3 * h, i].astype(F32) + held[3 * h + 1, i].astype(F32) + held[3 * h + 2, i].astype(F32)
            for i in range(3)
        ]
        sig = jax.nn.sigmoid(gate)
        made[h, 0] = (gate * sig * up).astype(BF16)
        made[h, 1] = (grad * up * sig * (1.0 + gate * (1.0 - sig))).astype(BF16)
        made[h, 2] = (grad * gate * sig).astype(BF16)
        writes[h].start()
    for write in writes:
        write.wait()


def middle(low, high):
    shape = low[0].shape
    out = jax.ShapeDtypeStruct(shape, BF16)
    size = low[0].size
    return pl.pallas_call(
        middle_kernel,
        in_specs=[ANY] * 6,
        out_specs=[ANY] * 2,
        out_shape=[out, out],
        scratch_shapes=[
            pltpu.VMEM((6, *shape), BF16),
            pltpu.VMEM((2, *shape), BF16),
            pltpu.SemaphoreType.DMA((6,)),
            pltpu.SemaphoreType.DMA((2,)),
        ],
        compiler_params=pltpu.CompilerParams(vmem_limit_bytes=VMEM_LIMIT),
        cost_estimate=pl.CostEstimate(flops=14 * size, bytes_accessed=16 * size, transcendentals=size),
        name="middle",
    )(*low, *high)


def second_kernel(places, has_prev, last, order, count_hbm, weight_hbm, *refs):
    halves, refs = refs[: 2 * len(places)], refs[2 * len(places) :]
    (grad_hbm, gate_hbm, up_hbm, down_hbm), refs = refs[:4], refs[4:]
    done_hbm, refs = refs[: len(last)], refs[len(last) :]
    refs = refs[1:] if has_prev else refs
    dg_hbm, refs = refs[0], refs[1:]
    outs, refs = (refs[:2], refs[2:]) if last else (refs[:1], refs[1:])
    (count_ref, weight_ref, work, grads, gates, ups, downs, out_acc, in_acc, rows_ref, stage), refs = (
        refs[:11],
        refs[11:],
    )
    if last:
        (keep_ref, send_ref, high, low, plain, total), refs = refs[:6], refs[6:]
        done, refs = refs[: len(last)], refs[len(last) :]
    data_sem, weight_sem, out_sem = refs
    rows, hidden = work.shape[2], work.shape[3]
    half, cut = rows // 2, hidden // 2
    experts = grads.shape[0]

    data_copies = [
        pltpu.make_async_copy(count_hbm, count_ref, data_sem.at[0]),
        pltpu.make_async_copy(weight_hbm, weight_ref, data_sem.at[1]),
        pltpu.make_async_copy(grad_hbm, grads, data_sem.at[2]),
    ]
    for q in range(2 * len(places)):
        data_copies.append(
            pltpu.make_async_copy(
                halves[q], work.at[q // 2, :, pl.ds(half * (q % 2), half)], data_sem.at[3 + q]
            )
        )
    done_copies = []
    for q in range(len(last)):
        done_copies.append(
            pltpu.make_async_copy(done_hbm[q], done[q], data_sem.at[3 + 2 * len(places) + q])
        )

    def read(k, turn, expert):
        i, c = turn // 2, turn % 2
        source, held = ((down_hbm, downs), (gate_hbm, gates), (up_hbm, ups))[k]
        size = held.shape[1] // 2
        part = pl.ds(pl.multiple_of(size * c, size), size)
        return pltpu.make_async_copy(
            source.at[expert, part], held.at[i, part], weight_sem.at[k, turn]
        )

    def expert_of(turn):
        i = turn // 2
        return order[2 * nth(places, i // 2) + i % 2]

    def ahead(k, turn, count):
        turn, k = turn + (k + count) // 3, (k + count) % 3

        @pl.when(turn < 2 * experts)
        def _():
            read(k, turn, expert_of(turn)).start()

    def writes(c, expert):
        return pltpu.make_async_copy(
            stage.at[c], dg_hbm.at[expert, pl.ds(pl.multiple_of(cut * c, cut), cut)], out_sem.at[c]
        )

    start(data_copies)
    for k in range(AHEAD):
        ahead(0, jnp.int32(0), k)
    start(done_copies)
    for copy in data_copies:
        copy.wait()

    if last:
        order_of = [p for group in last for p in group] + list(places)
        for slot, place in enumerate(order_of):
            scale, seen = 0.0, 0.0
            for e in range(2):
                at = 2 * place + e
                chosen = picks(count_ref, at, e, rows)
                scale = scale + jnp.where(chosen, weight_ref[at : at + 1, :], 0.0)
                seen = seen + chosen.astype(F32)
            part = scale.astype(BF16)
            high[slot] = part
            low[slot] = (scale - part.astype(F32)).astype(BF16)
            plain[slot] = seen.astype(BF16)

    def add(slot, out_rows, in_rows):
        out = dot(high[slot], out_rows, ((0,), (0,))) + dot(low[slot], out_rows, ((0,), (0,)))
        return out, dot(plain[slot], in_rows, ((0,), (0,)))

    def body(turn, carry):
        i, c = turn // 2, turn % 2
        which, end = i // 2, i % 2
        lanes = pl.ds(pl.multiple_of(cut * c, cut), cut)
        read(0, turn, 0).wait()
        ahead(0, turn, AHEAD)

        @pl.when(turn >= 2)
        def _():
            writes(c, 0).wait()

        stage[c] = dot(work[which, 0, :, lanes], grads[i], ((0,), (0,))).astype(BF16)
        writes(c, expert_of(turn)).start()
        out_part = dot(work[which, 0, :, lanes], downs[i, lanes], ((1,), (0,)))

        @pl.when(c == 0)
        def _():
            out_acc[...] = out_part

        @pl.when(c == 1)
        def _():
            out_acc[...] += out_part

        size = out_acc.shape[1] // 2
        wide = pl.ds(pl.multiple_of(size * c, size), size)
        read(1, turn, 0).wait()
        ahead(1, turn, AHEAD)
        in_acc[:, wide] = dot(work[which, 1], gates[i, wide], ((1,), (1,)))
        read(2, turn, 0).wait()
        ahead(2, turn, AHEAD)
        in_acc[:, wide] += dot(work[which, 2], ups[i, wide], ((1,), (1,)))

        @pl.when((c == 1) & (end == 0))
        def _():
            rows_ref[which, 0] = out_acc[...].astype(BF16)
            rows_ref[which, 1] = in_acc[...].astype(BF16)

        @pl.when((c == 1) & (end == 1))
        def _():
            at = 2 * nth(places, which) + 1
            own = jnp.max(picks(count_ref, at, 1, rows).astype(F32), axis=1, keepdims=True) > 0
            for k, value in enumerate((out_acc, in_acc)):
                before = rows_ref[which, k].astype(F32)
                rows_ref[which, k] = jnp.where(own, value[...], before).astype(BF16)

        if last:

            @pl.when(turn == 1)
            def _():
                for copy in done_copies:
                    copy.wait()
                slot = 0
                for d, group in zip(done, last):
                    for g in range(len(group)):
                        for k, value in enumerate(add(slot, d[g, 0], d[g, 1])):
                            total[k] = value if slot == 0 else total[k] + value
                        slot += 1

        return carry

    lax.fori_loop(0, 2 * experts, body, 0)
    if last:
        length = keep_ref.shape[2]
        for k, value in enumerate(add(len(order_of) - 1, rows_ref[0, 0], rows_ref[0, 1])):
            value = total[k] + value
            for j in range(keep_ref.shape[0]):
                keep_ref[j, k] = value[2 * j * length : (2 * j + 1) * length]
                send_ref[j, k] = value[(2 * j + 1) * length : (2 * j + 2) * length].astype(BF16)
        finals = [
            pltpu.make_async_copy(send_ref, outs[1], out_sem.at[3]),
            pltpu.make_async_copy(keep_ref, outs[0], out_sem.at[2]),
        ]
    else:
        finals = [pltpu.make_async_copy(rows_ref, outs[0], out_sem.at[2])]
    start(finals)
    for c in range(2):
        writes(c, 0).wait()
    for copy in finals:
        copy.wait()


def second(places, last, blocks, order, count, weight, halves, grad, w_gate, w_up, w_down, done, prev):
    local, width, hidden = w_gate.shape
    tokens = count.shape[1]
    rows = grad.shape[1]
    experts = 2 * len(places)
    operands = [order, count, weight, *halves, grad, w_gate, w_up, w_down, *done]
    aliases = {}
    if prev is not None:
        operands.append(prev)
        aliases = {len(operands) - 1: 0}
    row_shape = (len(places), 2, rows, width)
    scratch = [
        pltpu.VMEM(count.shape, F32),
        pltpu.VMEM(weight.shape, F32),
        pltpu.VMEM((len(places), 3, rows, hidden), BF16),
        pltpu.VMEM(grad.shape, BF16),
        pltpu.VMEM((experts, width, hidden), BF16),
        pltpu.VMEM((experts, width, hidden), BF16),
        pltpu.VMEM((experts, hidden, width), BF16),
        pltpu.VMEM((rows, width), F32),
        pltpu.VMEM((rows, width), F32),
        pltpu.VMEM(row_shape, BF16),
        pltpu.VMEM((2, hidden // 2, width), BF16),
    ]
    outs = [jax.ShapeDtypeStruct((local, hidden, width), BF16)]
    if last:
        shape = (blocks // 2, 2, tokens // blocks, width)
        outs += [jax.ShapeDtypeStruct(shape, F32), jax.ShapeDtypeStruct(shape, BF16)]
        scratch += [pltpu.VMEM(shape, F32), pltpu.VMEM(shape, BF16)]
        scratch += [pltpu.VMEM((local // 2, rows, tokens), BF16)] * 3
        scratch += [pltpu.VMEM((2, tokens, width), F32)]
        scratch += [pltpu.VMEM(d.shape, BF16) for d in done]
    else:
        outs += [jax.ShapeDtypeStruct(row_shape, BF16)]
    scratch += [
        pltpu.SemaphoreType.DMA((3 + experts + len(done),)),
        pltpu.SemaphoreType.DMA((3, 2 * experts)),
        pltpu.SemaphoreType.DMA((4,)),
    ]
    return pl.pallas_call(
        functools.partial(second_kernel, places, prev is not None, last),
        in_specs=[SMEM] + [ANY] * (len(operands) - 1),
        out_specs=[ANY] * len(outs),
        scratch_shapes=scratch,
        out_shape=outs,
        input_output_aliases=aliases,
        compiler_params=pltpu.CompilerParams(vmem_limit_bytes=VMEM_LIMIT),
        cost_estimate=pl.CostEstimate(
            flops=8 * experts * rows * width * hidden,
            bytes_accessed=8 * experts * width * hidden,
            transcendentals=0,
        ),
        name="second" + "".join(map(str, places)),
    )(*operands)


def exchange(rows, blocks, order, count, weight, parts, w_gate, w_up, w_down):
    args = (order, count, weight, parts, w_gate, w_up, w_down)
    side = functools.partial(xor_permute, axis="tensor", mask=1)
    other = functools.partial(xor_permute, axis="tensor", mask=2)

    low3, high3, grad3 = first((3,), rows, *args)
    from_side, from_other = side(low3), other(high3)
    low1, high1, low2, high2, grad12 = first((1, 2), rows, *args)
    side_low, other_high = side(low1), other(high2)

    joined_high, joined_low = join(high1, from_other, low2, from_side)
    side_high, other_low = side(joined_high), other(joined_low)
    low0, high0, grad0 = first((0,), rows, *args)
    own_low, own_high = middle((low0, side_low, other_low), (high0, side_high, other_high))

    low1, high2 = side(own_low), other(own_high)
    high1, low2 = side(own_high), other(own_low)
    low3, high3 = other(low1), side(high2)
    run = functools.partial(second, blocks=blocks, order=order, count=count, weight=weight,
                            w_gate=w_gate, w_up=w_up, w_down=w_down)
    dg, rows0 = run((0,), (), halves=(own_low, own_high), grad=grad0, done=(), prev=None)
    dg, rows12 = run((1, 2), (), halves=(low1, high1, low2, high2), grad=grad12, done=(), prev=dg)
    dg, keep, send = run((3,), ((0,), (1, 2)), halves=(low3, high3), grad=grad3,
                         done=(rows0, rows12), prev=dg)

    got = xor_permute(send, "expert", 1)
    total = keep[0] + got[0].astype(F32)
    for j in range(1, blocks // 2):
        piece = (keep[j] + got[j].astype(F32)).astype(BF16)
        total = total + xor_permute(piece, "expert", 2 * j).astype(F32)
    total = total.astype(BF16)
    return total[0], total[1], dg


def small(tokens, cotangent, expert_ids, route_weight, w_gate, w_up, w_down):
    blocks, slabs = lax.axis_size("expert"), lax.axis_size("tensor")
    local = w_gate.shape[0]
    experts = local * blocks
    length, top = expert_ids.shape
    capacity = 2 * length * top // experts
    most = 2 * capacity * blocks
    fewer = most * 3 // 4

    own = pack(tokens, cotangent, expert_ids, route_weight)
    even = [own] + [xor_permute(own, "expert", j) for j in range(2, blocks, 2)]
    odd = [xor_permute(v, "expert", 1) for v in even]
    parts = [v for both in zip(even, odd) for v in both]
    order, fits, count, weight = route(parts, top, experts, local, slabs, fewer)
    run = [
        functools.partial(exchange, rows, blocks, order, count, weight, parts, w_gate, w_up, w_down)
        for rows in (fewer, most)
    ]
    return lax.cond(fits[0] > 0, *run)


def large(tokens, cotangent, expert_ids, route_weight, w_gate, w_up, w_down):
    resident_specialists = w_gate.shape[0]
    experts = resident_specialists * lax.axis_size("expert")
    tok_count = expert_ids.shape[0]
    top_count = expert_ids.shape[1]
    capacity = 2 * tok_count * top_count // experts
    model_width = tokens.shape[1]
    flat_ids = expert_ids.reshape(-1)
    onehot = (flat_ids[:, None] == jnp.arange(experts, dtype=jnp.int32)[None, :]).astype(jnp.int32)
    before = jnp.cumsum(onehot, axis=0) - onehot
    slot_index = jnp.sum(before * onehot, axis=1)
    target = flat_ids * capacity + slot_index
    chosen = (target[:, None] == jnp.arange(experts * capacity, dtype=jnp.int32)[None, :]).astype(F32)
    chosen = chosen.reshape(tok_count, top_count, experts * capacity)
    expert_assignment = jnp.sum(chosen, axis=1)
    weighted = jnp.sum(chosen * route_weight[:, :, None], axis=1)
    token_send = jnp.dot(expert_assignment.T.astype(BF16), tokens, preferred_element_type=F32)
    token_send = token_send.astype(BF16).reshape(experts, capacity, model_width)
    gradient_outgoing = jnp.dot(
        weighted.T, cotangent, precision=lax.Precision.HIGHEST, preferred_element_type=F32
    )
    gradient_outgoing = gradient_outgoing.astype(BF16).reshape(experts, capacity, model_width)
    token_rows = lax.all_to_all(token_send, "expert", split_axis=0, concat_axis=1, tiled=True)
    grad_rows = lax.all_to_all(gradient_outgoing, "expert", split_axis=0, concat_axis=1, tiled=True)
    pre_gate = jnp.einsum("erd,edf->erf", token_rows, w_gate, preferred_element_type=F32)
    pre_up = jnp.einsum("erd,edf->erf", token_rows, w_up, preferred_element_type=F32)
    slice_breadth = w_gate.shape[2] // lax.axis_size("tensor")
    gate_sum = lax.psum(pre_gate.astype(BF16), "tensor").astype(F32)
    up_sum = lax.psum(pre_up.astype(BF16), "tensor").astype(F32)
    sigmoid_all = jax.nn.sigmoid(gate_sum)
    hidden = (gate_sum * sigmoid_all * up_sum).astype(BF16)
    out_rows = jnp.einsum("erf,efd->erd", hidden, w_down, preferred_element_type=F32).astype(BF16)
    down_grad = jnp.einsum("erf,erd->efd", hidden, grad_rows, preferred_element_type=F32)
    offset = lax.axis_index("tensor") * slice_breadth
    gate_part = lax.dynamic_slice_in_dim(gate_sum, offset, slice_breadth, 2)
    up_part = lax.dynamic_slice_in_dim(up_sum, offset, slice_breadth, 2)
    sigmoid_part = lax.dynamic_slice_in_dim(sigmoid_all, offset, slice_breadth, 2)
    hidden_term = jnp.einsum("erd,efd->erf", grad_rows, w_down, preferred_element_type=F32)
    hidden_grad = lax.psum_scatter(
        hidden_term.astype(BF16), "tensor", scatter_dimension=2, tiled=True
    ).astype(F32)
    gate_grad = (
        hidden_grad * up_part * sigmoid_part * (1.0 + gate_part * (1.0 - sigmoid_part))
    ).astype(BF16)
    up_grad = (hidden_grad * gate_part * sigmoid_part).astype(BF16)
    gate_piece = lax.all_gather(gate_grad, "tensor", axis=2, tiled=True)
    up_piece = lax.all_gather(up_grad, "tensor", axis=2, tiled=True)
    running = jnp.einsum("erf,edf->erd", gate_piece, w_gate, preferred_element_type=F32)
    input_rows = running + jnp.einsum("erf,edf->erd", up_piece, w_up, preferred_element_type=F32)
    input_rows = input_rows.astype(BF16)
    returned_out = lax.all_to_all(out_rows, "expert", split_axis=1, concat_axis=0, tiled=True)
    returned_in = lax.all_to_all(input_rows, "expert", split_axis=1, concat_axis=0, tiled=True)
    returned_out = returned_out.reshape(experts * capacity, model_width)
    returned_in = returned_in.reshape(experts * capacity, model_width)
    mixed_out = jnp.dot(
        weighted, returned_out, precision=lax.Precision.HIGHEST, preferred_element_type=F32
    )
    input_grad = jnp.dot(expert_assignment.astype(BF16), returned_in, preferred_element_type=F32)
    return mixed_out.astype(BF16), input_grad.astype(BF16), down_grad.astype(BF16)


def local(tokens, cotangent, expert_ids, route_weight, w_gate, w_up, w_down):
    blocks, slabs = lax.axis_size("expert"), lax.axis_size("tensor")
    pairs = w_gate.shape[0] == 2 * slabs and slabs == 4
    few = blocks <= 8 and blocks & (blocks - 1) == 0
    short = 4 * expert_ids.shape[1] <= expert_ids.shape[0] <= META
    body = small if pairs and few and short else large
    return body(tokens, cotangent, expert_ids, route_weight, w_gate, w_up, w_down)


def solution(mesh):
    return jax.shard_map(
        local,
        mesh=mesh,
        in_specs=(
            P("expert", "tensor"),
            P("expert", "tensor"),
            P("expert", None),
            P("expert", None),
            P("expert", "tensor", None),
            P("expert", "tensor", None),
            P("expert", None, "tensor"),
        ),
        out_specs=(P("expert", "tensor"), P("expert", "tensor"), P("expert", None, "tensor")),
        check_vma=False,
    )
```

```python
import functools
import jax
import jax.numpy as jnp
from jax import lax
from jax.experimental import pallas as pl
from jax.experimental.pallas import tpu as pltpu
from jax.sharding import PartitionSpec as P

BF16 = jnp.bfloat16
F32 = jnp.float32
VMEM_LIMIT = 50 << 20
META = 128
AHEAD = 3


def xor_permute(x, axis, mask):
    return lax.ppermute(x, axis, [(i, i ^ mask) for i in range(lax.axis_size(axis))])


def dot(a, b, contract):
    return lax.dot_general(a, b, ((contract[0], contract[1]), ((), ())), preferred_element_type=F32)


def whole(shape):
    return pl.BlockSpec(shape, lambda *_: (0,) * len(shape))


def pack_kernel(tokens_ref, grad_ref, ids_ref, weight_ref, out_ref):
    length, width = tokens_ref.shape
    out_ref[:, :width] = tokens_ref[...]
    out_ref[:, width : 2 * width] = grad_ref[...]
    weight = weight_ref[...]
    high = weight.astype(BF16).astype(F32)
    mid = (weight - high).astype(BF16).astype(F32)
    low = weight - high - mid
    fields = jnp.concatenate([ids_ref[...].astype(F32), high, mid, low], axis=0)
    if fields.shape[0] < length:
        fields = jnp.concatenate([fields, jnp.zeros((length - fields.shape[0], length), F32)], axis=0)
    fields = jnp.concatenate([fields, jnp.zeros((length, META - length), F32)], axis=1)
    out_ref[:, 2 * width :] = fields.astype(BF16)


def pack(tokens, cotangent, expert_ids, route_weight):
    length, width = tokens.shape
    return pl.pallas_call(
        pack_kernel,
        out_shape=jax.ShapeDtypeStruct((length, 2 * width + META), BF16),
        name="pack",
    )(tokens, cotangent, expert_ids.T, route_weight.T)


def route_kernel(blocks, top, experts, local, slabs, cap, *refs):
    metas, (order_ref, fits_ref, count_ref, weight_ref) = refs[:blocks], refs[blocks:]
    my_expert, my_slab = lax.axis_index("expert"), lax.axis_index("tensor")
    turned = jnp.concatenate([m[:, : m.shape[0]].astype(F32) for m in metas], axis=1)
    tokens = turned.shape[1]
    ids = turned[:top]
    weights = turned[top : 2 * top] + turned[2 * top : 3 * top] + turned[3 * top : 4 * top]

    all_names = lax.broadcasted_iota(jnp.int32, (experts, 1), 0).astype(F32)
    picked = jnp.zeros((experts, tokens), F32)
    for k in range(top):
        picked += (ids[k : k + 1] == all_names).astype(F32)
    down = jnp.sum(picked, axis=1, keepdims=True)
    across = dot(jnp.ones((8, tokens), BF16), picked.astype(BF16), ((1,), (1,)))[:1]
    row = lax.broadcasted_iota(jnp.int32, (experts, experts), 0)
    col = lax.broadcasted_iota(jnp.int32, (experts, experts), 1)
    same = row // local == col // local
    col_first = (across > down) | ((across == down) & (col < row))
    row_first = (down > across) | ((down == across) & (row < col))
    rank_down = jnp.sum((same & col_first).astype(F32), axis=1, keepdims=True)
    rank_across = jnp.sum((same & row_first).astype(F32), axis=0, keepdims=True)
    mate = same & (rank_across == (local - 1) - rank_down)
    pair = down + jnp.sum(jnp.where(mate, across, 0.0), axis=1, keepdims=True)
    fits_ref[0] = (jnp.max(pair) <= cap).astype(jnp.int32)

    names = (lax.broadcasted_iota(jnp.int32, (local, 1), 0) + my_expert * local).astype(F32)
    mine = jnp.zeros((local, tokens), F32)
    share = jnp.zeros((local, tokens), F32)
    for k in range(top):
        hit = ids[k : k + 1] == names
        mine += hit.astype(F32)
        share += jnp.where(hit, weights[k : k + 1], 0.0)
    earlier = (
        lax.broadcasted_iota(jnp.int32, (tokens, tokens), 0)
        < lax.broadcasted_iota(jnp.int32, (tokens, tokens), 1)
    ).astype(BF16)
    count = dot(mine.astype(BF16), earlier, ((1,), (0,)))
    count = jnp.where(mine > 0, count, -1.0)
    load = jnp.sum(mine, axis=1, keepdims=True)
    load_across = dot(jnp.ones((8, tokens), BF16), mine.astype(BF16), ((1,), (1,)))[:1]
    row = lax.broadcasted_iota(jnp.int32, (local, local), 0)
    col = lax.broadcasted_iota(jnp.int32, (local, local), 1)
    first = (load_across > load) | ((load_across == load) & (col < row))
    rank = jnp.sum(first.astype(F32), axis=1, keepdims=True)
    index = lax.broadcasted_iota(jnp.int32, (local, 1), 0).astype(F32)
    for place in range(slabs):
        slab = place ^ my_slab
        for end in range(2):
            wanted = (slab if end == 0 else local - 1 - slab).astype(F32)
            chosen = rank == wanted
            at = 2 * place + end
            order_ref[at] = jnp.sum(jnp.where(chosen, index, 0.0)).astype(jnp.int32)
            count_ref[at : at + 1] = jnp.sum(jnp.where(chosen, count, 0.0), axis=0, keepdims=True)
            weight_ref[at : at + 1] = jnp.sum(jnp.where(chosen, share, 0.0), axis=0, keepdims=True)


def route(parts, top, experts, local, slabs, cap):
    length, lanes = parts[0].shape
    tokens = length * len(parts)
    smem = pl.BlockSpec(memory_space=pltpu.SMEM)
    meta = pl.BlockSpec((length, META), lambda i: (0, lanes // META - 1))
    return pl.pallas_call(
        functools.partial(route_kernel, len(parts), top, experts, local, slabs, cap),
        grid=(1,),
        in_specs=[meta] * len(parts),
        out_specs=(smem, smem, whole((local, tokens)), whole((local, tokens))),
        compiler_params=pltpu.CompilerParams(vmem_limit_bytes=VMEM_LIMIT),
        out_shape=(
            jax.ShapeDtypeStruct((local,), jnp.int32),
            jax.ShapeDtypeStruct((1,), jnp.int32),
            jax.ShapeDtypeStruct((local, tokens), F32),
            jax.ShapeDtypeStruct((local, tokens), F32),
        ),
        name="route",
    )(*parts)


def picks(count_ref, at, end, rows):
    count = count_ref[pl.ds(at, 1), :]
    target = jnp.where(end == 0, count, jnp.where(count >= 0, (rows - 1) - count, -1.0))
    line = lax.broadcasted_iota(jnp.int32, (rows, count.shape[1]), 0).astype(F32)
    return line == target


ANY = pl.BlockSpec(memory_space=pl.ANY)
SMEM = pl.BlockSpec(memory_space=pltpu.SMEM)


def start(copies):
    for copy in copies:
        copy.start()


def first_kernel(places, blocks, order, count_hbm, weight_hbm, *refs):
    parts, refs = refs[:blocks], refs[blocks:]
    sources, refs = refs[:3], refs[3:]
    halves, refs = refs[: 2 * len(places)], refs[2 * len(places) :]
    grad_out, refs = refs[0], refs[1:]
    (count_ref, weight_ref, data, downs, gates, ups, rows_ref, turned_ref, sums, grads) = refs[:10]
    data_sem, weight_sem, out_sem = refs[10:]
    length = parts[0].shape[0]
    experts, rows, width = grads.shape
    half, cut = rows // 2, sums.shape[3] // 2

    small_copies = [
        pltpu.make_async_copy(count_hbm, count_ref, data_sem.at[blocks]),
        pltpu.make_async_copy(weight_hbm, weight_ref, data_sem.at[blocks + 1]),
    ] + [
        pltpu.make_async_copy(
            parts[j].at[:, : 2 * width], data.at[j * length : (j + 1) * length, :], data_sem.at[j]
        )
        for j in range(blocks)
    ]

    def read(k, end, which, expert):
        span = slice(width * end, width * (end + 1))
        if k == 0:
            held = downs.at[which, :, span]
        else:
            held = (gates, ups)[k - 1].at[which, span]
        return pltpu.make_async_copy(
            sources[k].at[expert], held, weight_sem.at[2 * k + end, which]
        )

    def ahead(turn, which):
        which, turn = which + turn // 6, turn % 6

        @pl.when(which < len(places))
        def _():
            end = turn % 2
            read(turn // 2, end, which, order[2 * nth(places, which) + end]).start()

    start(small_copies)
    for turn in range(AHEAD):
        ahead(turn, jnp.int32(0))
    for copy in small_copies:
        copy.wait()
    last = pltpu.make_async_copy(grads, grad_out, out_sem.at[2 * len(places)])

    def body(which, carry):
        at = 2 * nth(places, which)
        chosen = jnp.concatenate([picks(count_ref, at + e, e, rows) for e in range(2)], axis=0)
        share = jnp.concatenate(
            [jnp.broadcast_to(weight_ref[pl.ds(at + e, 1), :], chosen[:rows].shape) for e in range(2)],
            axis=0,
        )
        scale = jnp.sum(jnp.where(chosen, share, 0.0), axis=1, keepdims=True)
        select = chosen.astype(BF16)
        found = dot(select, data[:, :width], ((1,), (0,))).astype(BF16)
        back = (dot(select, data[:, width:], ((1,), (0,))) * scale).astype(BF16)
        for e in range(2):
            span = slice(width * e, width * (e + 1))
            rows_ref[:, span] = found[rows * e : rows * (e + 1)]
            turned_ref[:, span] = back[rows * e : rows * (e + 1)]
            grads[2 * which + e] = back[rows * e : rows * (e + 1)]

        @pl.when(which == len(places) - 1)
        def _():
            last.start()

        for k in range(3):
            for e in range(2):
                read(k, e, which, 0).wait()
                ahead(2 * k + e + AHEAD, which)

            def columns(c, carry):
                lanes = pl.ds(pl.multiple_of(cut * c, cut), cut)
                if k == 0:
                    value = dot(turned_ref[...], downs[which, lanes], ((1,), (1,)))
                else:
                    value = dot(rows_ref[...], (gates, ups)[k - 1][which, :, lanes], ((1,), (0,)))
                value = value.astype(BF16)
                for h in range(2):
                    sums[2 * which + h, (k + 2) % 3, :, lanes] = value[half * h : half * (h + 1)]
                return carry

            lax.fori_loop(0, 2, columns, 0)
            for p in range(len(places)):

                @pl.when(which == p)
                def _():
                    for h in range(2):
                        q, slot = 2 * p + h, (k + 2) % 3
                        pltpu.make_async_copy(
                            sums.at[q, slot], halves[q].at[slot], out_sem.at[q]
                        ).start()

        return carry

    lax.fori_loop(0, len(places), body, 0)
    for q in range(2 * len(places)):
        pltpu.make_async_copy(sums.at[q], halves[q], out_sem.at[q]).wait()
    last.wait()


def nth(places, which):
    value = places[0]
    for at in range(1, len(places)):
        value = jnp.where(which == at, places[at], value)
    return value


def first(places, rows, order, count, weight, parts, w_gate, w_up, w_down):
    _, width, hidden = w_gate.shape
    tokens = count.shape[1]
    experts = 2 * len(places)
    half = jax.ShapeDtypeStruct((3, rows // 2, hidden), BF16)
    return pl.pallas_call(
        functools.partial(first_kernel, places, len(parts)),
        in_specs=[SMEM] + [ANY] * (5 + len(parts)),
        out_specs=[ANY] * (experts + 1),
        scratch_shapes=[
            pltpu.VMEM(count.shape, F32),
            pltpu.VMEM(weight.shape, F32),
            pltpu.VMEM((tokens, 2 * width), BF16),
            pltpu.VMEM((len(places), hidden, 2 * width), BF16),
            pltpu.VMEM((len(places), 2 * width, hidden), BF16),
            pltpu.VMEM((len(places), 2 * width, hidden), BF16),
            pltpu.VMEM((rows, 2 * width), BF16),
            pltpu.VMEM((rows, 2 * width), BF16),
            pltpu.VMEM((experts, 3, rows // 2, hidden), BF16),
            pltpu.VMEM((experts, rows, width), BF16),
            pltpu.SemaphoreType.DMA((len(parts) + 2,)),
            pltpu.SemaphoreType.DMA((6, len(places))),
            pltpu.SemaphoreType.DMA((experts + 1,)),
        ],
        out_shape=[half] * experts + [jax.ShapeDtypeStruct((experts, rows, width), BF16)],
        compiler_params=pltpu.CompilerParams(vmem_limit_bytes=VMEM_LIMIT),
        cost_estimate=pl.CostEstimate(
            flops=6 * experts * rows * width * hidden,
            bytes_accessed=6 * experts * width * hidden,
            transcendentals=0,
        ),
        name="first" + "".join(map(str, places)),
    )(order, count, weight, *parts, w_down, w_gate, w_up)


def join_kernel(*refs):
    sources, outs, (held, made, in_sem, out_sem) = refs[:4], refs[4:6], refs[6:]
    reads = [pltpu.make_async_copy(sources[q], held.at[q], in_sem.at[q]) for q in range(4)]
    writes = [pltpu.make_async_copy(made.at[h], outs[h], out_sem.at[h]) for h in range(2)]
    start(reads)
    for h in range(2):
        for q in range(2 * h, 2 * h + 2):
            reads[q].wait()
        made[h] = (held[2 * h].astype(F32) + held[2 * h + 1].astype(F32)).astype(BF16)
        writes[h].start()
    for write in writes:
        write.wait()


def join(a, b, c, d):
    shape = jax.ShapeDtypeStruct(a.shape, a.dtype)
    return pl.pallas_call(
        join_kernel,
        in_specs=[ANY] * 4,
        out_specs=[ANY] * 2,
        out_shape=[shape, shape],
        scratch_shapes=[
            pltpu.VMEM((4, *a.shape), BF16),
            pltpu.VMEM((2, *a.shape), BF16),
            pltpu.SemaphoreType.DMA((4,)),
            pltpu.SemaphoreType.DMA((2,)),
        ],
        compiler_params=pltpu.CompilerParams(vmem_limit_bytes=VMEM_LIMIT),
        cost_estimate=pl.CostEstimate(flops=2 * a.size, bytes_accessed=12 * a.size, transcendentals=0),
        name="join",
    )(a, b, c, d)


def middle_kernel(*refs):
    sources, outs, (held, made, in_sem, out_sem) = refs[:6], refs[6:8], refs[8:]
    reads = [pltpu.make_async_copy(sources[q], held.at[q], in_sem.at[q]) for q in range(6)]
    writes = [pltpu.make_async_copy(made.at[h], outs[h], out_sem.at[h]) for h in range(2)]
    start(reads)
    for h in range(2):
        for q in range(3 * h, 3 * h + 3):
            reads[q].wait()
        gate, up, grad = [
            held[3 * h, i].astype(F32) + held[3 * h + 1, i].astype(F32) + held[3 * h + 2, i].astype(F32)
            for i in range(3)
        ]
        sig = jax.nn.sigmoid(gate)
        made[h, 0] = (gate * sig * up).astype(BF16)
        made[h, 1] = (grad * up * sig * (1.0 + gate * (1.0 - sig))).astype(BF16)
        made[h, 2] = (grad * gate * sig).astype(BF16)
        writes[h].start()
    for write in writes:
        write.wait()


def middle(low, high):
    shape = low[0].shape
    out = jax.ShapeDtypeStruct(shape, BF16)
    size = low[0].size
    return pl.pallas_call(
        middle_kernel,
        in_specs=[ANY] * 6,
        out_specs=[ANY] * 2,
        out_shape=[out, out],
        scratch_shapes=[
            pltpu.VMEM((6, *shape), BF16),
            pltpu.VMEM((2, *shape), BF16),
            pltpu.SemaphoreType.DMA((6,)),
            pltpu.SemaphoreType.DMA((2,)),
        ],
        compiler_params=pltpu.CompilerParams(vmem_limit_bytes=VMEM_LIMIT),
        cost_estimate=pl.CostEstimate(flops=14 * size, bytes_accessed=16 * size, transcendentals=size),
        name="middle",
    )(*low, *high)


def second_kernel(places, has_prev, last, order, count_hbm, weight_hbm, *refs):
    halves, refs = refs[: 2 * len(places)], refs[2 * len(places) :]
    (grad_hbm, gate_hbm, up_hbm, down_hbm), refs = refs[:4], refs[4:]
    done_hbm, refs = refs[: len(last)], refs[len(last) :]
    refs = refs[1:] if has_prev else refs
    dg_hbm, refs = refs[0], refs[1:]
    outs, refs = (refs[:2], refs[2:]) if last else (refs[:1], refs[1:])
    (count_ref, weight_ref, work, grads, gates, ups, downs, out_acc, in_acc, rows_ref, stage), refs = (
        refs[:11],
        refs[11:],
    )
    if last:
        (keep_ref, send_ref, high, low, plain, total), refs = refs[:6], refs[6:]
        done, refs = refs[: len(last)], refs[len(last) :]
    data_sem, weight_sem, out_sem = refs
    rows, hidden = work.shape[2], work.shape[3]
    half, cut = rows // 2, hidden // 2
    experts = grads.shape[0]

    data_copies = [
        pltpu.make_async_copy(count_hbm, count_ref, data_sem.at[0]),
        pltpu.make_async_copy(weight_hbm, weight_ref, data_sem.at[1]),
        pltpu.make_async_copy(grad_hbm, grads, data_sem.at[2]),
    ]
    for q in range(2 * len(places)):
        data_copies.append(
            pltpu.make_async_copy(
                halves[q], work.at[q // 2, :, pl.ds(half * (q % 2), half)], data_sem.at[3 + q]
            )
        )
    done_copies = []
    for q in range(len(last)):
        done_copies.append(
            pltpu.make_async_copy(done_hbm[q], done[q], data_sem.at[3 + 2 * len(places) + q])
        )

    def read(k, turn, expert):
        i, c = turn // 2, turn % 2
        source, held = ((down_hbm, downs), (gate_hbm, gates), (up_hbm, ups))[k]
        size = held.shape[1] // 2
        part = pl.ds(pl.multiple_of(size * c, size), size)
        return pltpu.make_async_copy(
            source.at[expert, part], held.at[i, part], weight_sem.at[k, turn]
        )

    def expert_of(turn):
        i = turn // 2
        return order[2 * nth(places, i // 2) + i % 2]

    def ahead(k, turn, count):
        turn, k = turn + (k + count) // 3, (k + count) % 3

        @pl.when(turn < 2 * experts)
        def _():
            read(k, turn, expert_of(turn)).start()

    def writes(c, expert):
        return pltpu.make_async_copy(
            stage.at[c], dg_hbm.at[expert, pl.ds(pl.multiple_of(cut * c, cut), cut)], out_sem.at[c]
        )

    start(data_copies)
    for k in range(AHEAD):
        ahead(0, jnp.int32(0), k)
    start(done_copies)
    for copy in data_copies:
        copy.wait()

    if last:
        order_of = [p for group in last for p in group] + list(places)
        for slot, place in enumerate(order_of):
            scale, seen = 0.0, 0.0
            for e in range(2):
                at = 2 * place + e
                chosen = picks(count_ref, at, e, rows)
                scale = scale + jnp.where(chosen, weight_ref[at : at + 1, :], 0.0)
                seen = seen + chosen.astype(F32)
            part = scale.astype(BF16)
            high[slot] = part
            low[slot] = (scale - part.astype(F32)).astype(BF16)
            plain[slot] = seen.astype(BF16)

    def add(slot, out_rows, in_rows):
        out = dot(high[slot], out_rows, ((0,), (0,))) + dot(low[slot], out_rows, ((0,), (0,)))
        return out, dot(plain[slot], in_rows, ((0,), (0,)))

    def body(turn, carry):
        i, c = turn // 2, turn % 2
        which, end = i // 2, i % 2
        lanes = pl.ds(pl.multiple_of(cut * c, cut), cut)
        read(0, turn, 0).wait()
        ahead(0, turn, AHEAD)

        @pl.when(turn >= 2)
        def _():
            writes(c, 0).wait()

        stage[c] = dot(work[which, 0, :, lanes], grads[i], ((0,), (0,))).astype(BF16)
        writes(c, expert_of(turn)).start()
        out_part = dot(work[which, 0, :, lanes], downs[i, lanes], ((1,), (0,)))

        @pl.when(c == 0)
        def _():
            out_acc[...] = out_part

        @pl.when(c == 1)
        def _():
            out_acc[...] += out_part

        size = out_acc.shape[1] // 2
        wide = pl.ds(pl.multiple_of(size * c, size), size)
        read(1, turn, 0).wait()
        ahead(1, turn, AHEAD)
        in_acc[:, wide] = dot(work[which, 1], gates[i, wide], ((1,), (1,)))
        read(2, turn, 0).wait()
        ahead(2, turn, AHEAD)
        in_acc[:, wide] += dot(work[which, 2], ups[i, wide], ((1,), (1,)))

        @pl.when((c == 1) & (end == 0))
        def _():
            rows_ref[which, 0] = out_acc[...].astype(BF16)
            rows_ref[which, 1] = in_acc[...].astype(BF16)

        @pl.when((c == 1) & (end == 1))
        def _():
            at = 2 * nth(places, which) + 1
            own = jnp.max(picks(count_ref, at, 1, rows).astype(F32), axis=1, keepdims=True) > 0
            for k, value in enumerate((out_acc, in_acc)):
                before = rows_ref[which, k].astype(F32)
                rows_ref[which, k] = jnp.where(own, value[...], before).astype(BF16)

        if last:

            @pl.when(turn == 1)
            def _():
                for copy in done_copies:
                    copy.wait()
                slot = 0
                for d, group in zip(done, last):
                    for g in range(len(group)):
                        for k, value in enumerate(add(slot, d[g, 0], d[g, 1])):
                            total[k] = value if slot == 0 else total[k] + value
                        slot += 1

        return carry

    lax.fori_loop(0, 2 * experts, body, 0)
    if last:
        length = keep_ref.shape[2]
        for k, value in enumerate(add(len(order_of) - 1, rows_ref[0, 0], rows_ref[0, 1])):
            value = total[k] + value
            for j in range(keep_ref.shape[0]):
                keep_ref[j, k] = value[2 * j * length : (2 * j + 1) * length].astype(BF16)
                send_ref[j, k] = value[(2 * j + 1) * length : (2 * j + 2) * length].astype(BF16)
        finals = [
            pltpu.make_async_copy(send_ref, outs[1], out_sem.at[3]),
            pltpu.make_async_copy(keep_ref, outs[0], out_sem.at[2]),
        ]
    else:
        finals = [pltpu.make_async_copy(rows_ref, outs[0], out_sem.at[2])]
    start(finals)
    for c in range(2):
        writes(c, 0).wait()
    for copy in finals:
        copy.wait()


def second(places, last, blocks, order, count, weight, halves, grad, w_gate, w_up, w_down, done, prev):
    local, width, hidden = w_gate.shape
    tokens = count.shape[1]
    rows = grad.shape[1]
    experts = 2 * len(places)
    operands = [order, count, weight, *halves, grad, w_gate, w_up, w_down, *done]
    aliases = {}
    if prev is not None:
        operands.append(prev)
        aliases = {len(operands) - 1: 0}
    row_shape = (len(places), 2, rows, width)
    scratch = [
        pltpu.VMEM(count.shape, F32),
        pltpu.VMEM(weight.shape, F32),
        pltpu.VMEM((len(places), 3, rows, hidden), BF16),
        pltpu.VMEM(grad.shape, BF16),
        pltpu.VMEM((experts, width, hidden), BF16),
        pltpu.VMEM((experts, width, hidden), BF16),
        pltpu.VMEM((experts, hidden, width), BF16),
        pltpu.VMEM((rows, width), F32),
        pltpu.VMEM((rows, width), F32),
        pltpu.VMEM(row_shape, BF16),
        pltpu.VMEM((2, hidden // 2, width), BF16),
    ]
    outs = [jax.ShapeDtypeStruct((local, hidden, width), BF16)]
    if last:
        shape = (blocks // 2, 2, tokens // blocks, width)
        outs += [jax.ShapeDtypeStruct(shape, BF16)] * 2
        scratch += [pltpu.VMEM(shape, BF16)] * 2
        scratch += [pltpu.VMEM((local // 2, rows, tokens), BF16)] * 3
        scratch += [pltpu.VMEM((2, tokens, width), F32)]
        scratch += [pltpu.VMEM(d.shape, BF16) for d in done]
    else:
        outs += [jax.ShapeDtypeStruct(row_shape, BF16)]
    scratch += [
        pltpu.SemaphoreType.DMA((3 + experts + len(done),)),
        pltpu.SemaphoreType.DMA((3, 2 * experts)),
        pltpu.SemaphoreType.DMA((4,)),
    ]
    return pl.pallas_call(
        functools.partial(second_kernel, places, prev is not None, last),
        in_specs=[SMEM] + [ANY] * (len(operands) - 1),
        out_specs=[ANY] * len(outs),
        scratch_shapes=scratch,
        out_shape=outs,
        input_output_aliases=aliases,
        compiler_params=pltpu.CompilerParams(vmem_limit_bytes=VMEM_LIMIT),
        cost_estimate=pl.CostEstimate(
            flops=8 * experts * rows * width * hidden,
            bytes_accessed=8 * experts * width * hidden,
            transcendentals=0,
        ),
        name="second" + "".join(map(str, places)),
    )(*operands)


def exchange(rows, blocks, order, count, weight, parts, w_gate, w_up, w_down):
    args = (order, count, weight, parts, w_gate, w_up, w_down)
    side = functools.partial(xor_permute, axis="tensor", mask=1)
    other = functools.partial(xor_permute, axis="tensor", mask=2)

    low3, high3, grad3 = first((3,), rows, *args)
    from_side, from_other = side(low3), other(high3)
    low1, high1, low2, high2, grad12 = first((1, 2), rows, *args)
    side_low, other_high = side(low1), other(high2)

    joined_high, joined_low = join(high1, from_other, low2, from_side)
    side_high, other_low = side(joined_high), other(joined_low)
    low0, high0, grad0 = first((0,), rows, *args)
    own_low, own_high = middle((low0, side_low, other_low), (high0, side_high, other_high))

    low1, high2 = side(own_low), other(own_high)
    high1, low2 = side(own_high), other(own_low)
    low3, high3 = other(low1), side(high2)
    run = functools.partial(second, blocks=blocks, order=order, count=count, weight=weight,
                            w_gate=w_gate, w_up=w_up, w_down=w_down)
    dg, rows0 = run((0,), (), halves=(own_low, own_high), grad=grad0, done=(), prev=None)
    dg, rows12 = run((1, 2), (), halves=(low1, high1, low2, high2), grad=grad12, done=(), prev=dg)
    dg, keep, send = run((3,), ((0,), (1, 2)), halves=(low3, high3), grad=grad3,
                         done=(rows0, rows12), prev=dg)

    got = xor_permute(send, "expert", 1)
    total = keep[0].astype(F32) + got[0].astype(F32)
    for j in range(1, blocks // 2):
        piece = (keep[j].astype(F32) + got[j].astype(F32)).astype(BF16)
        total = total + xor_permute(piece, "expert", 2 * j).astype(F32)
    total = total.astype(BF16)
    return total[0], total[1], dg


def small(tokens, cotangent, expert_ids, route_weight, w_gate, w_up, w_down):
    blocks, slabs = lax.axis_size("expert"), lax.axis_size("tensor")
    local = w_gate.shape[0]
    experts = local * blocks
    length, top = expert_ids.shape
    capacity = 2 * length * top // experts
    most = 2 * capacity * blocks
    fewer = most * 3 // 4

    own = pack(tokens, cotangent, expert_ids, route_weight)
    even = [own] + [xor_permute(own, "expert", j) for j in range(2, blocks, 2)]
    odd = [xor_permute(v, "expert", 1) for v in even]
    parts = [v for both in zip(even, odd) for v in both]
    order, fits, count, weight = route(parts, top, experts, local, slabs, fewer)
    run = [
        functools.partial(exchange, rows, blocks, order, count, weight, parts, w_gate, w_up, w_down)
        for rows in (fewer, most)
    ]
    return lax.cond(fits[0] > 0, *run)


def large(tokens, cotangent, expert_ids, route_weight, w_gate, w_up, w_down):
    resident_specialists = w_gate.shape[0]
    experts = resident_specialists * lax.axis_size("expert")
    tok_count = expert_ids.shape[0]
    top_count = expert_ids.shape[1]
    capacity = 2 * tok_count * top_count // experts
    model_width = tokens.shape[1]
    flat_ids = expert_ids.reshape(-1)
    onehot = (flat_ids[:, None] == jnp.arange(experts, dtype=jnp.int32)[None, :]).astype(jnp.int32)
    before = jnp.cumsum(onehot, axis=0) - onehot
    slot_index = jnp.sum(before * onehot, axis=1)
    target = flat_ids * capacity + slot_index
    chosen = (target[:, None] == jnp.arange(experts * capacity, dtype=jnp.int32)[None, :]).astype(F32)
    chosen = chosen.reshape(tok_count, top_count, experts * capacity)
    expert_assignment = jnp.sum(chosen, axis=1)
    weighted = jnp.sum(chosen * route_weight[:, :, None], axis=1)
    token_send = jnp.dot(expert_assignment.T.astype(BF16), tokens, preferred_element_type=F32)
    token_send = token_send.astype(BF16).reshape(experts, capacity, model_width)
    gradient_outgoing = jnp.dot(
        weighted.T, cotangent, precision=lax.Precision.HIGHEST, preferred_element_type=F32
    )
    gradient_outgoing = gradient_outgoing.astype(BF16).reshape(experts, capacity, model_width)
    token_rows = lax.all_to_all(token_send, "expert", split_axis=0, concat_axis=1, tiled=True)
    grad_rows = lax.all_to_all(gradient_outgoing, "expert", split_axis=0, concat_axis=1, tiled=True)
    pre_gate = jnp.einsum("erd,edf->erf", token_rows, w_gate, preferred_element_type=F32)
    pre_up = jnp.einsum("erd,edf->erf", token_rows, w_up, preferred_element_type=F32)
    slice_breadth = w_gate.shape[2] // lax.axis_size("tensor")
    gate_sum = lax.psum(pre_gate.astype(BF16), "tensor").astype(F32)
    up_sum = lax.psum(pre_up.astype(BF16), "tensor").astype(F32)
    sigmoid_all = jax.nn.sigmoid(gate_sum)
    hidden = (gate_sum * sigmoid_all * up_sum).astype(BF16)
    out_rows = jnp.einsum("erf,efd->erd", hidden, w_down, preferred_element_type=F32).astype(BF16)
    down_grad = jnp.einsum("erf,erd->efd", hidden, grad_rows, preferred_element_type=F32)
    offset = lax.axis_index("tensor") * slice_breadth
    gate_part = lax.dynamic_slice_in_dim(gate_sum, offset, slice_breadth, 2)
    up_part = lax.dynamic_slice_in_dim(up_sum, offset, slice_breadth, 2)
    sigmoid_part = lax.dynamic_slice_in_dim(sigmoid_all, offset, slice_breadth, 2)
    hidden_term = jnp.einsum("erd,efd->erf", grad_rows, w_down, preferred_element_type=F32)
    hidden_grad = lax.psum_scatter(
        hidden_term.astype(BF16), "tensor", scatter_dimension=2, tiled=True
    ).astype(F32)
    gate_grad = (
        hidden_grad * up_part * sigmoid_part * (1.0 + gate_part * (1.0 - sigmoid_part))
    ).astype(BF16)
    up_grad = (hidden_grad * gate_part * sigmoid_part).astype(BF16)
    gate_piece = lax.all_gather(gate_grad, "tensor", axis=2, tiled=True)
    up_piece = lax.all_gather(up_grad, "tensor", axis=2, tiled=True)
    running = jnp.einsum("erf,edf->erd", gate_piece, w_gate, preferred_element_type=F32)
    input_rows = running + jnp.einsum("erf,edf->erd", up_piece, w_up, preferred_element_type=F32)
    input_rows = input_rows.astype(BF16)
    returned_out = lax.all_to_all(out_rows, "expert", split_axis=1, concat_axis=0, tiled=True)
    returned_in = lax.all_to_all(input_rows, "expert", split_axis=1, concat_axis=0, tiled=True)
    returned_out = returned_out.reshape(experts * capacity, model_width)
    returned_in = returned_in.reshape(experts * capacity, model_width)
    mixed_out = jnp.dot(
        weighted, returned_out, precision=lax.Precision.HIGHEST, preferred_element_type=F32
    )
    input_grad = jnp.dot(expert_assignment.astype(BF16), returned_in, preferred_element_type=F32)
    return mixed_out.astype(BF16), input_grad.astype(BF16), down_grad.astype(BF16)


def local(tokens, cotangent, expert_ids, route_weight, w_gate, w_up, w_down):
    blocks, slabs = lax.axis_size("expert"), lax.axis_size("tensor")
    pairs = w_gate.shape[0] == 2 * slabs and slabs == 4
    few = blocks <= 8 and blocks & (blocks - 1) == 0
    short = 4 * expert_ids.shape[1] <= expert_ids.shape[0] <= META
    body = small if pairs and few and short else large
    return body(tokens, cotangent, expert_ids, route_weight, w_gate, w_up, w_down)


def solution(mesh):
    return jax.shard_map(
        local,
        mesh=mesh,
        in_specs=(
            P("expert", "tensor"),
            P("expert", "tensor"),
            P("expert", None),
            P("expert", None),
            P("expert", "tensor", None),
            P("expert", "tensor", None),
            P("expert", None, "tensor"),
        ),
        out_specs=(P("expert", "tensor"), P("expert", "tensor"), P("expert", None, "tensor")),
        check_vma=False,
    )
```

```python
import functools
import math
import jax
import jax.numpy as jnp
from jax import lax
from jax.experimental import pallas as pl
from jax.experimental.pallas import tpu as pltpu
from jax.sharding import PartitionSpec as P

BF16 = jnp.bfloat16
F32 = jnp.float32
VMEM_LIMIT = 16 << 20
META = 128
AHEAD = 3


def xor_permute(x, axis, mask):
    return lax.ppermute(x, axis, [(i, i ^ mask) for i in range(lax.axis_size(axis))])


def dot(a, b, contract):
    return lax.dot_general(a, b, ((contract[0], contract[1]), ((), ())), preferred_element_type=F32)


def whole(shape):
    return pl.BlockSpec(shape, lambda *_: (0,) * len(shape))


def pack_kernel(tokens_ref, grad_ref, ids_ref, weight_ref, out_ref):
    length, width = tokens_ref.shape
    out_ref[:, :width] = tokens_ref[...]
    out_ref[:, width : 2 * width] = grad_ref[...]
    weight = weight_ref[...]
    high = weight.astype(BF16).astype(F32)
    mid = (weight - high).astype(BF16).astype(F32)
    low = weight - high - mid
    fields = jnp.concatenate([ids_ref[...].astype(F32), high, mid, low], axis=0)
    if fields.shape[0] < length:
        fields = jnp.concatenate([fields, jnp.zeros((length - fields.shape[0], length), F32)], axis=0)
    fields = jnp.concatenate([fields, jnp.zeros((length, META - length), F32)], axis=1)
    out_ref[:, 2 * width :] = fields.astype(BF16)


def pack(tokens, cotangent, expert_ids, route_weight):
    length, width = tokens.shape
    return pl.pallas_call(
        pack_kernel,
        out_shape=jax.ShapeDtypeStruct((length, 2 * width + META), BF16),
        name="pack",
    )(tokens, cotangent, expert_ids.T, route_weight.T)


def route_kernel(blocks, top, experts, local, slabs, cap, *refs):
    metas, (order_ref, fits_ref, count_ref, weight_ref) = refs[:blocks], refs[blocks:]
    my_expert, my_slab = lax.axis_index("expert"), lax.axis_index("tensor")
    turned = jnp.concatenate([m[:, : m.shape[0]].astype(F32) for m in metas], axis=1)
    tokens = turned.shape[1]
    ids = turned[:top]
    weights = turned[top : 2 * top] + turned[2 * top : 3 * top] + turned[3 * top : 4 * top]

    all_names = lax.broadcasted_iota(jnp.int32, (experts, 1), 0).astype(F32)
    picked = jnp.zeros((experts, tokens), F32)
    for k in range(top):
        picked += (ids[k : k + 1] == all_names).astype(F32)
    down = jnp.sum(picked, axis=1, keepdims=True)
    across = dot(jnp.ones((8, tokens), BF16), picked.astype(BF16), ((1,), (1,)))[:1]
    row = lax.broadcasted_iota(jnp.int32, (experts, experts), 0)
    col = lax.broadcasted_iota(jnp.int32, (experts, experts), 1)
    same = row // local == col // local
    col_first = (across > down) | ((across == down) & (col < row))
    row_first = (down > across) | ((down == across) & (row < col))
    rank_down = jnp.sum((same & col_first).astype(F32), axis=1, keepdims=True)
    rank_across = jnp.sum((same & row_first).astype(F32), axis=0, keepdims=True)
    mate = same & (rank_across == (local - 1) - rank_down)
    pair = down + jnp.sum(jnp.where(mate, across, 0.0), axis=1, keepdims=True)
    fits_ref[0] = (jnp.max(pair) <= cap).astype(jnp.int32)

    names = (lax.broadcasted_iota(jnp.int32, (local, 1), 0) + my_expert * local).astype(F32)
    mine = jnp.zeros((local, tokens), F32)
    share = jnp.zeros((local, tokens), F32)
    for k in range(top):
        hit = ids[k : k + 1] == names
        mine += hit.astype(F32)
        share += jnp.where(hit, weights[k : k + 1], 0.0)
    earlier = (
        lax.broadcasted_iota(jnp.int32, (tokens, tokens), 0)
        < lax.broadcasted_iota(jnp.int32, (tokens, tokens), 1)
    ).astype(BF16)
    count = dot(mine.astype(BF16), earlier, ((1,), (0,)))
    count = jnp.where(mine > 0, count, -1.0)
    load = jnp.sum(mine, axis=1, keepdims=True)
    load_across = dot(jnp.ones((8, tokens), BF16), mine.astype(BF16), ((1,), (1,)))[:1]
    row = lax.broadcasted_iota(jnp.int32, (local, local), 0)
    col = lax.broadcasted_iota(jnp.int32, (local, local), 1)
    first = (load_across > load) | ((load_across == load) & (col < row))
    rank = jnp.sum(first.astype(F32), axis=1, keepdims=True)
    index = lax.broadcasted_iota(jnp.int32, (local, 1), 0).astype(F32)
    for place in range(slabs):
        slab = place ^ my_slab
        for end in range(2):
            wanted = (slab if end == 0 else local - 1 - slab).astype(F32)
            chosen = rank == wanted
            at = 2 * place + end
            order_ref[at] = jnp.sum(jnp.where(chosen, index, 0.0)).astype(jnp.int32)
            count_ref[at : at + 1] = jnp.sum(jnp.where(chosen, count, 0.0), axis=0, keepdims=True)
            weight_ref[at : at + 1] = jnp.sum(jnp.where(chosen, share, 0.0), axis=0, keepdims=True)


def route(parts, top, experts, local, slabs, cap):
    length, lanes = parts[0].shape
    tokens = length * len(parts)
    smem = pl.BlockSpec(memory_space=pltpu.SMEM)
    meta = pl.BlockSpec((length, META), lambda i: (0, lanes // META - 1))
    return pl.pallas_call(
        functools.partial(route_kernel, len(parts), top, experts, local, slabs, cap),
        grid=(1,),
        in_specs=[meta] * len(parts),
        out_specs=(smem, smem, whole((local, tokens)), whole((local, tokens))),
        compiler_params=pltpu.CompilerParams(vmem_limit_bytes=VMEM_LIMIT),
        out_shape=(
            jax.ShapeDtypeStruct((local,), jnp.int32),
            jax.ShapeDtypeStruct((1,), jnp.int32),
            jax.ShapeDtypeStruct((local, tokens), F32),
            jax.ShapeDtypeStruct((local, tokens), F32),
        ),
        name="route",
    )(*parts)


def picks(count_ref, at, end, rows):
    count = count_ref[pl.ds(at, 1), :]
    target = jnp.where(end == 0, count, jnp.where(count >= 0, (rows - 1) - count, -1.0))
    line = lax.broadcasted_iota(jnp.int32, (rows, count.shape[1]), 0).astype(F32)
    return line == target


ANY = pl.BlockSpec(memory_space=pl.ANY)
SMEM = pl.BlockSpec(memory_space=pltpu.SMEM)


def grant(scratch):
    sizes = [math.prod(m.shape) * jnp.dtype(m.dtype).itemsize for m in scratch if m.memory_space == pltpu.VMEM]
    return sum(sizes) + (8 << 20)


def start(copies):
    for copy in copies:
        copy.start()


def first_kernel(places, blocks, order, count_hbm, weight_hbm, *refs):
    parts, refs = refs[:blocks], refs[blocks:]
    sources, refs = refs[:3], refs[3:]
    halves, refs = refs[: 2 * len(places)], refs[2 * len(places) :]
    grad_out, refs = refs[0], refs[1:]
    (count_ref, weight_ref, data, downs, gates, ups, rows_ref, turned_ref, sums, grads) = refs[:10]
    data_sem, weight_sem, out_sem = refs[10:]
    length = parts[0].shape[0]
    experts, rows, width = grads.shape
    half, cut = rows // 2, sums.shape[3] // 2

    small_copies = [
        pltpu.make_async_copy(count_hbm, count_ref, data_sem.at[blocks]),
        pltpu.make_async_copy(weight_hbm, weight_ref, data_sem.at[blocks + 1]),
    ] + [
        pltpu.make_async_copy(
            parts[j].at[:, : 2 * width], data.at[j * length : (j + 1) * length, :], data_sem.at[j]
        )
        for j in range(blocks)
    ]

    def read(k, end, which, expert):
        span = slice(width * end, width * (end + 1))
        if k == 0:
            held = downs.at[which, :, span]
        else:
            held = (gates, ups)[k - 1].at[which, span]
        return pltpu.make_async_copy(
            sources[k].at[expert], held, weight_sem.at[2 * k + end, which]
        )

    def ahead(turn, which):
        which, turn = which + turn // 6, turn % 6

        @pl.when(which < len(places))
        def _():
            end = turn % 2
            read(turn // 2, end, which, order[2 * nth(places, which) + end]).start()

    start(small_copies)
    for turn in range(AHEAD):
        ahead(turn, jnp.int32(0))
    for copy in small_copies:
        copy.wait()
    last = pltpu.make_async_copy(grads, grad_out, out_sem.at[2 * len(places)])

    def body(which, carry):
        at = 2 * nth(places, which)
        chosen = jnp.concatenate([picks(count_ref, at + e, e, rows) for e in range(2)], axis=0)
        share = jnp.concatenate(
            [jnp.broadcast_to(weight_ref[pl.ds(at + e, 1), :], chosen[:rows].shape) for e in range(2)],
            axis=0,
        )
        scale = jnp.sum(jnp.where(chosen, share, 0.0), axis=1, keepdims=True)
        select = chosen.astype(BF16)
        found = dot(select, data[:, :width], ((1,), (0,))).astype(BF16)
        back = (dot(select, data[:, width:], ((1,), (0,))) * scale).astype(BF16)
        for e in range(2):
            span = slice(width * e, width * (e + 1))
            rows_ref[:, span] = found[rows * e : rows * (e + 1)]
            turned_ref[:, span] = back[rows * e : rows * (e + 1)]
            grads[2 * which + e] = back[rows * e : rows * (e + 1)]

        @pl.when(which == len(places) - 1)
        def _():
            last.start()

        for k in range(3):
            for e in range(2):
                read(k, e, which, 0).wait()
                ahead(2 * k + e + AHEAD, which)

            def columns(c, carry):
                lanes = pl.ds(pl.multiple_of(cut * c, cut), cut)
                if k == 0:
                    value = dot(turned_ref[...], downs[which, lanes], ((1,), (1,)))
                else:
                    value = dot(rows_ref[...], (gates, ups)[k - 1][which, :, lanes], ((1,), (0,)))
                value = value.astype(BF16)
                for h in range(2):
                    sums[2 * which + h, (k + 2) % 3, :, lanes] = value[half * h : half * (h + 1)]
                return carry

            lax.fori_loop(0, 2, columns, 0)
            for p in range(len(places)):

                @pl.when(which == p)
                def _():
                    for h in range(2):
                        q, slot = 2 * p + h, (k + 2) % 3
                        pltpu.make_async_copy(
                            sums.at[q, slot], halves[q].at[slot], out_sem.at[q]
                        ).start()

        return carry

    lax.fori_loop(0, len(places), body, 0)
    for q in range(2 * len(places)):
        pltpu.make_async_copy(sums.at[q], halves[q], out_sem.at[q]).wait()
    last.wait()


def nth(places, which):
    value = places[0]
    for at in range(1, len(places)):
        value = jnp.where(which == at, places[at], value)
    return value


def first(places, rows, order, count, weight, parts, w_gate, w_up, w_down):
    _, width, hidden = w_gate.shape
    tokens = count.shape[1]
    experts = 2 * len(places)
    half = jax.ShapeDtypeStruct((3, rows // 2, hidden), BF16)
    scratch = [
        pltpu.VMEM(count.shape, F32),
        pltpu.VMEM(weight.shape, F32),
        pltpu.VMEM((tokens, 2 * width), BF16),
        pltpu.VMEM((len(places), hidden, 2 * width), BF16),
        pltpu.VMEM((len(places), 2 * width, hidden), BF16),
        pltpu.VMEM((len(places), 2 * width, hidden), BF16),
        pltpu.VMEM((rows, 2 * width), BF16),
        pltpu.VMEM((rows, 2 * width), BF16),
        pltpu.VMEM((experts, 3, rows // 2, hidden), BF16),
        pltpu.VMEM((experts, rows, width), BF16),
        pltpu.SemaphoreType.DMA((len(parts) + 2,)),
        pltpu.SemaphoreType.DMA((6, len(places))),
        pltpu.SemaphoreType.DMA((experts + 1,)),
    ]
    return pl.pallas_call(
        functools.partial(first_kernel, places, len(parts)),
        in_specs=[SMEM] + [ANY] * (5 + len(parts)),
        out_specs=[ANY] * (experts + 1),
        scratch_shapes=scratch,
        out_shape=[half] * experts + [jax.ShapeDtypeStruct((experts, rows, width), BF16)],
        compiler_params=pltpu.CompilerParams(vmem_limit_bytes=grant(scratch)),
        cost_estimate=pl.CostEstimate(
            flops=6 * experts * rows * width * hidden,
            bytes_accessed=6 * experts * width * hidden,
            transcendentals=0,
        ),
        name="first" + "".join(map(str, places)),
    )(order, count, weight, *parts, w_down, w_gate, w_up)


def join_kernel(*refs):
    sources, outs, (held, made, in_sem, out_sem) = refs[:4], refs[4:6], refs[6:]
    reads = [pltpu.make_async_copy(sources[q], held.at[q], in_sem.at[q]) for q in range(4)]
    writes = [pltpu.make_async_copy(made.at[h], outs[h], out_sem.at[h]) for h in range(2)]
    start(reads)
    for h in range(2):
        for q in range(2 * h, 2 * h + 2):
            reads[q].wait()
        made[h] = (held[2 * h].astype(F32) + held[2 * h + 1].astype(F32)).astype(BF16)
        writes[h].start()
    for write in writes:
        write.wait()


def join(a, b, c, d):
    shape = jax.ShapeDtypeStruct(a.shape, a.dtype)
    return pl.pallas_call(
        join_kernel,
        in_specs=[ANY] * 4,
        out_specs=[ANY] * 2,
        out_shape=[shape, shape],
        scratch_shapes=[
            pltpu.VMEM((4, *a.shape), BF16),
            pltpu.VMEM((2, *a.shape), BF16),
            pltpu.SemaphoreType.DMA((4,)),
            pltpu.SemaphoreType.DMA((2,)),
        ],
        compiler_params=pltpu.CompilerParams(vmem_limit_bytes=VMEM_LIMIT),
        cost_estimate=pl.CostEstimate(flops=2 * a.size, bytes_accessed=12 * a.size, transcendentals=0),
        name="join",
    )(a, b, c, d)


def middle_kernel(*refs):
    sources, outs, (held, made, in_sem, out_sem) = refs[:6], refs[6:8], refs[8:]
    reads = [pltpu.make_async_copy(sources[q], held.at[q], in_sem.at[q]) for q in range(6)]
    writes = [pltpu.make_async_copy(made.at[h], outs[h], out_sem.at[h]) for h in range(2)]
    start(reads)
    for h in range(2):
        for q in range(3 * h, 3 * h + 3):
            reads[q].wait()
        gate, up, grad = [
            held[3 * h, i].astype(F32) + held[3 * h + 1, i].astype(F32) + held[3 * h + 2, i].astype(F32)
            for i in range(3)
        ]
        sig = jax.nn.sigmoid(gate)
        made[h, 0] = (gate * sig * up).astype(BF16)
        made[h, 1] = (grad * up * sig * (1.0 + gate * (1.0 - sig))).astype(BF16)
        made[h, 2] = (grad * gate * sig).astype(BF16)
        writes[h].start()
    for write in writes:
        write.wait()


def middle(low, high):
    shape = low[0].shape
    out = jax.ShapeDtypeStruct(shape, BF16)
    size = low[0].size
    return pl.pallas_call(
        middle_kernel,
        in_specs=[ANY] * 6,
        out_specs=[ANY] * 2,
        out_shape=[out, out],
        scratch_shapes=[
            pltpu.VMEM((6, *shape), BF16),
            pltpu.VMEM((2, *shape), BF16),
            pltpu.SemaphoreType.DMA((6,)),
            pltpu.SemaphoreType.DMA((2,)),
        ],
        compiler_params=pltpu.CompilerParams(vmem_limit_bytes=VMEM_LIMIT),
        cost_estimate=pl.CostEstimate(flops=14 * size, bytes_accessed=16 * size, transcendentals=size),
        name="middle",
    )(*low, *high)


def second_kernel(places, has_prev, last, order, count_hbm, weight_hbm, *refs):
    halves, refs = refs[: 2 * len(places)], refs[2 * len(places) :]
    (grad_hbm, gate_hbm, up_hbm, down_hbm), refs = refs[:4], refs[4:]
    done_hbm, refs = refs[: len(last)], refs[len(last) :]
    refs = refs[1:] if has_prev else refs
    dg_hbm, refs = refs[0], refs[1:]
    outs, refs = (refs[:2], refs[2:]) if last else (refs[:1], refs[1:])
    (count_ref, weight_ref, work, grads, gates, ups, downs, out_acc, in_acc, rows_ref, stage), refs = (
        refs[:11],
        refs[11:],
    )
    if last:
        (keep_ref, send_ref, high, low, plain, total), refs = refs[:6], refs[6:]
        done, refs = refs[: len(last)], refs[len(last) :]
    data_sem, weight_sem, out_sem = refs
    rows, hidden = work.shape[2], work.shape[3]
    half, cut = rows // 2, hidden // 2
    experts = grads.shape[0]

    data_copies = [
        pltpu.make_async_copy(count_hbm, count_ref, data_sem.at[0]),
        pltpu.make_async_copy(weight_hbm, weight_ref, data_sem.at[1]),
        pltpu.make_async_copy(grad_hbm, grads, data_sem.at[2]),
    ]
    for q in range(2 * len(places)):
        data_copies.append(
            pltpu.make_async_copy(
                halves[q], work.at[q // 2, :, pl.ds(half * (q % 2), half)], data_sem.at[3 + q]
            )
        )
    done_copies = []
    for q in range(len(last)):
        done_copies.append(
            pltpu.make_async_copy(done_hbm[q], done[q], data_sem.at[3 + 2 * len(places) + q])
        )

    def read(k, turn, expert):
        i, c = turn // 2, turn % 2
        source, held = ((down_hbm, downs), (gate_hbm, gates), (up_hbm, ups))[k]
        size = held.shape[1] // 2
        part = pl.ds(pl.multiple_of(size * c, size), size)
        return pltpu.make_async_copy(
            source.at[expert, part], held.at[i, part], weight_sem.at[k, turn]
        )

    def expert_of(turn):
        i = turn // 2
        return order[2 * nth(places, i // 2) + i % 2]

    def ahead(k, turn, count):
        turn, k = turn + (k + count) // 3, (k + count) % 3

        @pl.when(turn < 2 * experts)
        def _():
            read(k, turn, expert_of(turn)).start()

    def writes(c, expert):
        return pltpu.make_async_copy(
            stage.at[c], dg_hbm.at[expert, pl.ds(pl.multiple_of(cut * c, cut), cut)], out_sem.at[c]
        )

    start(data_copies)
    for k in range(AHEAD):
        ahead(0, jnp.int32(0), k)
    start(done_copies)
    for copy in data_copies:
        copy.wait()

    if last:
        order_of = [p for group in last for p in group] + list(places)
        for slot, place in enumerate(order_of):
            scale, seen = 0.0, 0.0
            for e in range(2):
                at = 2 * place + e
                chosen = picks(count_ref, at, e, rows)
                scale = scale + jnp.where(chosen, weight_ref[at : at + 1, :], 0.0)
                seen = seen + chosen.astype(F32)
            part = scale.astype(BF16)
            high[slot] = part
            low[slot] = (scale - part.astype(F32)).astype(BF16)
            plain[slot] = seen.astype(BF16)

    def add(slot, out_rows, in_rows):
        out = dot(high[slot], out_rows, ((0,), (0,))) + dot(low[slot], out_rows, ((0,), (0,)))
        return out, dot(plain[slot], in_rows, ((0,), (0,)))

    def body(turn, carry):
        i, c = turn // 2, turn % 2
        which, end = i // 2, i % 2
        lanes = pl.ds(pl.multiple_of(cut * c, cut), cut)
        read(0, turn, 0).wait()
        ahead(0, turn, AHEAD)

        @pl.when(turn >= 2)
        def _():
            writes(c, 0).wait()

        stage[c] = dot(work[which, 0, :, lanes], grads[i], ((0,), (0,))).astype(BF16)
        writes(c, expert_of(turn)).start()
        out_part = dot(work[which, 0, :, lanes], downs[i, lanes], ((1,), (0,)))

        @pl.when(c == 0)
        def _():
            out_acc[...] = out_part

        @pl.when(c == 1)
        def _():
            out_acc[...] += out_part

        size = out_acc.shape[1] // 2
        wide = pl.ds(pl.multiple_of(size * c, size), size)
        read(1, turn, 0).wait()
        ahead(1, turn, AHEAD)
        in_acc[:, wide] = dot(work[which, 1], gates[i, wide], ((1,), (1,)))
        read(2, turn, 0).wait()
        ahead(2, turn, AHEAD)
        in_acc[:, wide] += dot(work[which, 2], ups[i, wide], ((1,), (1,)))

        @pl.when((c == 1) & (end == 0))
        def _():
            rows_ref[which, 0] = out_acc[...].astype(BF16)
            rows_ref[which, 1] = in_acc[...].astype(BF16)

        @pl.when((c == 1) & (end == 1))
        def _():
            at = 2 * nth(places, which) + 1
            own = jnp.max(picks(count_ref, at, 1, rows).astype(F32), axis=1, keepdims=True) > 0
            for k, value in enumerate((out_acc, in_acc)):
                before = rows_ref[which, k].astype(F32)
                rows_ref[which, k] = jnp.where(own, value[...], before).astype(BF16)

        if last:

            @pl.when(turn == 1)
            def _():
                for copy in done_copies:
                    copy.wait()
                slot = 0
                for d, group in zip(done, last):
                    for g in range(len(group)):
                        for k, value in enumerate(add(slot, d[g, 0], d[g, 1])):
                            total[k] = value if slot == 0 else total[k] + value
                        slot += 1

        return carry

    lax.fori_loop(0, 2 * experts, body, 0)
    if last:
        length = keep_ref.shape[2]
        for k, value in enumerate(add(len(order_of) - 1, rows_ref[0, 0], rows_ref[0, 1])):
            value = total[k] + value
            for j in range(keep_ref.shape[0]):
                keep_ref[j, k] = value[2 * j * length : (2 * j + 1) * length].astype(BF16)
                send_ref[j, k] = value[(2 * j + 1) * length : (2 * j + 2) * length].astype(BF16)
        finals = [
            pltpu.make_async_copy(send_ref, outs[1], out_sem.at[3]),
            pltpu.make_async_copy(keep_ref, outs[0], out_sem.at[2]),
        ]
    else:
        finals = [pltpu.make_async_copy(rows_ref, outs[0], out_sem.at[2])]
    start(finals)
    for c in range(2):
        writes(c, 0).wait()
    for copy in finals:
        copy.wait()


def second(places, last, blocks, order, count, weight, halves, grad, w_gate, w_up, w_down, done, prev):
    local, width, hidden = w_gate.shape
    tokens = count.shape[1]
    rows = grad.shape[1]
    experts = 2 * len(places)
    operands = [order, count, weight, *halves, grad, w_gate, w_up, w_down, *done]
    aliases = {}
    if prev is not None:
        operands.append(prev)
        aliases = {len(operands) - 1: 0}
    row_shape = (len(places), 2, rows, width)
    scratch = [
        pltpu.VMEM(count.shape, F32),
        pltpu.VMEM(weight.shape, F32),
        pltpu.VMEM((len(places), 3, rows, hidden), BF16),
        pltpu.VMEM(grad.shape, BF16),
        pltpu.VMEM((experts, width, hidden), BF16),
        pltpu.VMEM((experts, width, hidden), BF16),
        pltpu.VMEM((experts, hidden, width), BF16),
        pltpu.VMEM((rows, width), F32),
        pltpu.VMEM((rows, width), F32),
        pltpu.VMEM(row_shape, BF16),
        pltpu.VMEM((2, hidden // 2, width), BF16),
    ]
    outs = [jax.ShapeDtypeStruct((local, hidden, width), BF16)]
    if last:
        shape = (blocks // 2, 2, tokens // blocks, width)
        outs += [jax.ShapeDtypeStruct(shape, BF16)] * 2
        scratch += [pltpu.VMEM(shape, BF16)] * 2
        scratch += [pltpu.VMEM((local // 2, rows, tokens), BF16)] * 3
        scratch += [pltpu.VMEM((2, tokens, width), F32)]
        scratch += [pltpu.VMEM(d.shape, BF16) for d in done]
    else:
        outs += [jax.ShapeDtypeStruct(row_shape, BF16)]
    scratch += [
        pltpu.SemaphoreType.DMA((3 + experts + len(done),)),
        pltpu.SemaphoreType.DMA((3, 2 * experts)),
        pltpu.SemaphoreType.DMA((4,)),
    ]
    return pl.pallas_call(
        functools.partial(second_kernel, places, prev is not None, last),
        in_specs=[SMEM] + [ANY] * (len(operands) - 1),
        out_specs=[ANY] * len(outs),
        scratch_shapes=scratch,
        out_shape=outs,
        input_output_aliases=aliases,
        compiler_params=pltpu.CompilerParams(vmem_limit_bytes=grant(scratch)),
        cost_estimate=pl.CostEstimate(
            flops=8 * experts * rows * width * hidden,
            bytes_accessed=8 * experts * width * hidden,
            transcendentals=0,
        ),
        name="second" + "".join(map(str, places)),
    )(*operands)


def exchange(rows, blocks, order, count, weight, parts, w_gate, w_up, w_down):
    args = (order, count, weight, parts, w_gate, w_up, w_down)
    side = functools.partial(xor_permute, axis="tensor", mask=1)
    other = functools.partial(xor_permute, axis="tensor", mask=2)

    low3, high3, grad3 = first((3,), rows, *args)
    from_side, from_other = side(low3), other(high3)
    low1, high1, low2, high2, grad12 = first((1, 2), rows, *args)
    side_low, other_high = side(low1), other(high2)

    joined_high, joined_low = join(high1, from_other, low2, from_side)
    side_high, other_low = side(joined_high), other(joined_low)
    low0, high0, grad0 = first((0,), rows, *args)
    own_low, own_high = middle((low0, side_low, other_low), (high0, side_high, other_high))

    low1, high2 = side(own_low), other(own_high)
    high1, low2 = side(own_high), other(own_low)
    low3, high3 = other(low1), side(high2)
    run = functools.partial(second, blocks=blocks, order=order, count=count, weight=weight,
                            w_gate=w_gate, w_up=w_up, w_down=w_down)
    dg, rows0 = run((0,), (), halves=(own_low, own_high), grad=grad0, done=(), prev=None)
    dg, rows12 = run((1, 2), (), halves=(low1, high1, low2, high2), grad=grad12, done=(), prev=dg)
    dg, keep, send = run((3,), ((0,), (1, 2)), halves=(low3, high3), grad=grad3,
                         done=(rows0, rows12), prev=dg)

    got = xor_permute(send, "expert", 1)
    total = keep[0].astype(F32) + got[0].astype(F32)
    for j in range(1, blocks // 2):
        piece = (keep[j].astype(F32) + got[j].astype(F32)).astype(BF16)
        total = total + xor_permute(piece, "expert", 2 * j).astype(F32)
    total = total.astype(BF16)
    return total[0], total[1], dg


def small(tokens, cotangent, expert_ids, route_weight, w_gate, w_up, w_down):
    blocks, slabs = lax.axis_size("expert"), lax.axis_size("tensor")
    local = w_gate.shape[0]
    experts = local * blocks
    length, top = expert_ids.shape
    capacity = 2 * length * top // experts
    most = 2 * capacity * blocks
    fewer = most * 3 // 4

    own = pack(tokens, cotangent, expert_ids, route_weight)
    even = [own] + [xor_permute(own, "expert", j) for j in range(2, blocks, 2)]
    odd = [xor_permute(v, "expert", 1) for v in even]
    parts = [v for both in zip(even, odd) for v in both]
    order, fits, count, weight = route(parts, top, experts, local, slabs, fewer)
    run = [
        functools.partial(exchange, rows, blocks, order, count, weight, parts, w_gate, w_up, w_down)
        for rows in (fewer, most)
    ]
    return lax.cond(fits[0] > 0, *run)


def large(tokens, cotangent, expert_ids, route_weight, w_gate, w_up, w_down):
    resident_specialists = w_gate.shape[0]
    experts = resident_specialists * lax.axis_size("expert")
    tok_count = expert_ids.shape[0]
    top_count = expert_ids.shape[1]
    capacity = 2 * tok_count * top_count // experts
    model_width = tokens.shape[1]
    flat_ids = expert_ids.reshape(-1)
    onehot = (flat_ids[:, None] == jnp.arange(experts, dtype=jnp.int32)[None, :]).astype(jnp.int32)
    before = jnp.cumsum(onehot, axis=0) - onehot
    slot_index = jnp.sum(before * onehot, axis=1)
    target = flat_ids * capacity + slot_index
    chosen = (target[:, None] == jnp.arange(experts * capacity, dtype=jnp.int32)[None, :]).astype(F32)
    chosen = chosen.reshape(tok_count, top_count, experts * capacity)
    expert_assignment = jnp.sum(chosen, axis=1)
    weighted = jnp.sum(chosen * route_weight[:, :, None], axis=1)
    token_send = jnp.dot(expert_assignment.T.astype(BF16), tokens, preferred_element_type=F32)
    token_send = token_send.astype(BF16).reshape(experts, capacity, model_width)
    gradient_outgoing = jnp.dot(
        weighted.T, cotangent, precision=lax.Precision.HIGHEST, preferred_element_type=F32
    )
    gradient_outgoing = gradient_outgoing.astype(BF16).reshape(experts, capacity, model_width)
    token_rows = lax.all_to_all(token_send, "expert", split_axis=0, concat_axis=1, tiled=True)
    grad_rows = lax.all_to_all(gradient_outgoing, "expert", split_axis=0, concat_axis=1, tiled=True)
    pre_gate = jnp.einsum("erd,edf->erf", token_rows, w_gate, preferred_element_type=F32)
    pre_up = jnp.einsum("erd,edf->erf", token_rows, w_up, preferred_element_type=F32)
    slice_breadth = w_gate.shape[2] // lax.axis_size("tensor")
    gate_sum = lax.psum(pre_gate.astype(BF16), "tensor").astype(F32)
    up_sum = lax.psum(pre_up.astype(BF16), "tensor").astype(F32)
    sigmoid_all = jax.nn.sigmoid(gate_sum)
    hidden = (gate_sum * sigmoid_all * up_sum).astype(BF16)
    out_rows = jnp.einsum("erf,efd->erd", hidden, w_down, preferred_element_type=F32).astype(BF16)
    down_grad = jnp.einsum("erf,erd->efd", hidden, grad_rows, preferred_element_type=F32)
    offset = lax.axis_index("tensor") * slice_breadth
    gate_part = lax.dynamic_slice_in_dim(gate_sum, offset, slice_breadth, 2)
    up_part = lax.dynamic_slice_in_dim(up_sum, offset, slice_breadth, 2)
    sigmoid_part = lax.dynamic_slice_in_dim(sigmoid_all, offset, slice_breadth, 2)
    hidden_term = jnp.einsum("erd,efd->erf", grad_rows, w_down, preferred_element_type=F32)
    hidden_grad = lax.psum_scatter(
        hidden_term.astype(BF16), "tensor", scatter_dimension=2, tiled=True
    ).astype(F32)
    gate_grad = (
        hidden_grad * up_part * sigmoid_part * (1.0 + gate_part * (1.0 - sigmoid_part))
    ).astype(BF16)
    up_grad = (hidden_grad * gate_part * sigmoid_part).astype(BF16)
    gate_piece = lax.all_gather(gate_grad, "tensor", axis=2, tiled=True)
    up_piece = lax.all_gather(up_grad, "tensor", axis=2, tiled=True)
    running = jnp.einsum("erf,edf->erd", gate_piece, w_gate, preferred_element_type=F32)
    input_rows = running + jnp.einsum("erf,edf->erd", up_piece, w_up, preferred_element_type=F32)
    input_rows = input_rows.astype(BF16)
    returned_out = lax.all_to_all(out_rows, "expert", split_axis=1, concat_axis=0, tiled=True)
    returned_in = lax.all_to_all(input_rows, "expert", split_axis=1, concat_axis=0, tiled=True)
    returned_out = returned_out.reshape(experts * capacity, model_width)
    returned_in = returned_in.reshape(experts * capacity, model_width)
    mixed_out = jnp.dot(
        weighted, returned_out, precision=lax.Precision.HIGHEST, preferred_element_type=F32
    )
    input_grad = jnp.dot(expert_assignment.astype(BF16), returned_in, preferred_element_type=F32)
    return mixed_out.astype(BF16), input_grad.astype(BF16), down_grad.astype(BF16)


def local(tokens, cotangent, expert_ids, route_weight, w_gate, w_up, w_down):
    blocks, slabs = lax.axis_size("expert"), lax.axis_size("tensor")
    pairs = w_gate.shape[0] == 2 * slabs and slabs == 4
    few = blocks <= 8 and blocks & (blocks - 1) == 0
    short = 4 * expert_ids.shape[1] <= expert_ids.shape[0] <= META
    body = small if pairs and few and short else large
    return body(tokens, cotangent, expert_ids, route_weight, w_gate, w_up, w_down)


def solution(mesh):
    return jax.shard_map(
        local,
        mesh=mesh,
        in_specs=(
            P("expert", "tensor"),
            P("expert", "tensor"),
            P("expert", None),
            P("expert", None),
            P("expert", "tensor", None),
            P("expert", "tensor", None),
            P("expert", None, "tensor"),
        ),
        out_specs=(P("expert", "tensor"), P("expert", "tensor"), P("expert", None, "tensor")),
        check_vma=False,
    )
```
